32 devices in a mesh: grp: 1, fsdp: 32 (over z, y, x, core), rep: 1.
Axes of the slice: x: 2, y: 2, z: 4, core: 2. Of those that a mesh axis runs over, the one named last changes fastest.
Arguments:
- items: bfloat16 [1, 16384, 512], P('rep', ('grp', 'fsdp')), may hold values from -30 to 30, as said below
- w_in: bfloat16 [512, 2048], P('fsdp'), may hold values from -0.25 to 0.25
- w_out: bfloat16 [2048, 1024], P('fsdp'), may hold values from -0.125 to 0.125
- users: bfloat16 [1, 1024, 1024], P('rep', ('grp', 'fsdp')), may hold values from -0.19921875 to 0.19921875
- res_codes: int32 [1, 16384, 1024], P('rep', ('grp', 'fsdp')), may hold values from 0 to 15
- range_idx: int32 [1024], P('grp'), may hold values from 0 to 3
- range_lo: float32 [4], P('grp'), may hold values from -1 to 1
- range_step: float32 [4], P('grp'), may hold values from 0.05 to 0.2
Outputs:
- new_codes: bfloat16 [1, 16384, 1024], P('rep', ('grp', 'fsdp'))
- best: float32 [1, 1024], P('rep', ('grp', 'fsdp'))
The draws below stay inside these ranges and needn't reach their ends.
Inputs may be any that keep to these rules, and one draw needn't show every extreme that they name: `items`: item features of order one.
All inputs are finite; a program needn't handle non-finite values.
Results may differ from the reference program's by a relative error of at most 0.0075.
Values may be sent and summed in bfloat16 or wider, within the bound.
No kernel may reach another device: no remote copies, remote signals or barrier semaphores. Data moves between devices by JAX's collectives and lax.ppermute only.
A program may use at most 64 MiB of HBM per device.

```python
import math
import jax
import jax.numpy as jnp
from jax import lax

D_IN = 512
HID = 2048
D = 1024
LEVELS = 4
REP_CLASSES = 1
ITEMS_CLASS = 16384
RES_CLASS = 16384
USERS_CLASS = 1024


def draw_items(key, part):
    shape = (REP_CLASSES, ITEMS_CLASS, D_IN)
    key_base, key_rows, key_cols = jax.random.split(jax.random.fold_in(key, 11), 3)
    rows = jnp.exp(jax.random.uniform(key_rows, (REP_CLASSES, ITEMS_CLASS, 1), jnp.float32, jnp.log(0.3), jnp.log(3.0)))
    cols = jnp.exp(jax.random.uniform(key_cols, (1, 1, D_IN), jnp.float32, jnp.log(0.3), jnp.log(3.0)))
    values = jax.random.normal(key_base, shape, jnp.float32) * rows * cols
    return jnp.clip(values, -30.0, 30.0).astype(jnp.bfloat16)


def plant(values, own_key, least, largest):
    longest = values.shape.index(max(values.shape))
    spots = []
    for shift in (0, 1):
        where = [jax.random.randint(jax.random.fold_in(own_key, axis), (), 0, length) for axis, length in enumerate(values.shape)]
        where[longest] = (where[longest] + shift) % values.shape[longest]
        spots.append(tuple(where))
    return values.at[spots[0]].set(least).at[spots[1]].set(largest)


def block_levels(own_key, extent, cuts, low, high):
    loudness, own = 1.0, jax.random.fold_in(own_key, 6)
    for axis_at, parts in cuts:
        draws = jnp.exp(jax.random.uniform(jax.random.fold_in(own, axis_at), (parts,), jnp.float32, low / len(cuts), high / len(cuts)))
        loudness = loudness * jnp.repeat(draws, extent[axis_at] // parts).reshape([-1 if axis == axis_at else 1 for axis in range(len(extent))])
    return loudness


def bell_draw(stream_key, extent, spread, most, cuts=(), held_as=jnp.bfloat16):
    drawn = jax.random.normal(stream_key, extent, jnp.float32) * spread
    if len(cuts) > 0:
        drawn = block_levels(stream_key, extent, cuts, -0.22, 0.18) * drawn
    return jnp.clip(drawn, min=-most, max=most).astype(held_as)


def setup_inputs(seed: int = 0, part: int = 0) -> dict:
    key_of = jax.random.split(jax.random.key(seed), 9)
    part_splits = jax.random.split(jax.random.fold_in(key_of[8], part), 9)
    return {
        "items": draw_items(jax.random.fold_in(jax.random.fold_in(key_of[8], part), 71), part),
        "w_in": bell_draw(key_of[1], (D_IN, HID), D_IN ** -0.5, 0.25, ((0, 32),)),
        "w_out": bell_draw(key_of[2], (HID, D), HID ** -0.5, 0.125, ((0, 32),)),
        "users": bell_draw(part_splits[3], (REP_CLASSES, USERS_CLASS, D), 0.03125, 0.19921875, ((1, 32),)),
        "res_codes": plant(jax.random.randint(part_splits[4], (REP_CLASSES, RES_CLASS, D), 0, 16), jax.random.fold_in(part_splits[4], 1), 0, 15).astype(jnp.int32),
        "range_idx": plant(jax.random.randint(part_splits[5], (D,), 0, LEVELS), jax.random.fold_in(part_splits[5], 1), 0, LEVELS - 1).astype(jnp.int32),
        "range_lo": jnp.clip(jax.random.uniform(part_splits[6], (LEVELS,), jnp.float32, -1.0, 1.0), -1.0, 1.0),
        "range_step": jnp.clip(jnp.exp(jax.random.uniform(part_splits[7], (LEVELS,), jnp.float32, math.log(0.05), math.log(0.2))), 0.05, 0.2),
    }


def tower(rows, w_in, w_out):
    hidden = jax.nn.silu(jnp.dot(rows, w_in, preferred_element_type=jnp.float32)).astype(jnp.bfloat16)
    return jnp.dot(hidden, w_out, preferred_element_type=jnp.float32)


def reference(items, w_in, w_out, users, res_codes, range_idx, range_lo, range_step):
    embed = lax.map(lambda rows: tower(rows, w_in, w_out), items)
    upper = jnp.max(embed, axis=(0, 1))
    lower = jnp.min(embed, axis=(0, 1))
    mid = (upper + lower) * 0.5
    half = (upper - lower) * 0.5
    new_codes = (7.5 * (embed - mid) / (half + 1e-5)).astype(jnp.bfloat16)
    levels = jnp.arange(LEVELS, dtype=jnp.int32)
    match = (range_idx[None, :] == levels[:, None]).astype(jnp.float32)
    step_d = jnp.sum(range_step[:, None] * match, axis=0)
    lo_d = jnp.sum(range_lo[:, None] * match, axis=0)

    def class_best(pair):
        member, codes = pair
        folded = (member.astype(jnp.float32) * step_d).astype(jnp.bfloat16)
        offset = jnp.dot(member.astype(jnp.float32), lo_d, precision=lax.Precision.HIGHEST)
        scores = jnp.dot(codes.astype(jnp.bfloat16), folded.T, preferred_element_type=jnp.float32)
        return jnp.max(scores, axis=0) + offset

    best = lax.map(class_best, (users, res_codes))
    return new_codes, best
```

```python
import functools

import jax
import jax.numpy as jnp
from jax import lax
from jax.experimental import pallas as pl
from jax.experimental.pallas import tpu as pltpu
from jax.sharding import PartitionSpec as P

ANY = pl.BlockSpec(memory_space=pl.ANY)
VMEM = pl.BlockSpec(memory_space=pltpu.VMEM)
SMEM = pl.BlockSpec(memory_space=pltpu.SMEM)
BF16 = jnp.bfloat16
F32 = jnp.float32
MIB = 1 << 20


def swap(x, axis, n, k):
    return lax.ppermute(x, axis, [(i, i ^ k) for i in range(n)])


def chip_and_core():
    me = lax.axis_index("fsdp")
    return me // 2, me % 2


def place(pieces, keys, rows, target, sems):
    chip, _ = chip_and_core()
    copies = []
    for piece, chips in zip(pieces, keys):
        for slot, key in enumerate(chips):
            copies.append(
                pltpu.make_async_copy(
                    piece.at[pl.ds(slot * rows, rows), :],
                    target.at[pl.ds(pl.multiple_of((chip ^ key) * rows, rows), rows), :],
                    sems.at[len(copies)],
                )
            )
    for copy in copies:
        copy.start()
    return copies


def score_kernel(
    keys, idx, lo, step, own, other, u0, u1, u2, u3, best, members, sems
):
    pieces = (u0, u1, u2, u3)
    rows = u0.shape[0] // 4
    copies = place(pieces, keys, rows, members, sems)
    index = idx[...]
    step_d = jnp.zeros(index.shape, F32)
    lo_d = jnp.zeros(index.shape, F32)
    for level in range(lo.shape[0]):
        step_d = jnp.where(index == level, step[level], step_d)
        lo_d = jnp.where(index == level, lo[level], lo_d)
    high = lo_d.astype(BF16)
    rest = lo_d - high.astype(F32)
    middle = rest.astype(BF16)
    low = (rest - middle.astype(F32)).astype(BF16)
    row = lax.broadcasted_iota(jnp.int32, (16, index.shape[1]), 0)
    parts = jnp.where(
        row == 0,
        high.astype(F32),
        jnp.where(row == 1, middle.astype(F32), jnp.where(row == 2, low.astype(F32), 0.0)),
    ).astype(BF16)
    for copy in copies:
        copy.wait()
    contract = (((1,), (1,)), ((), ()))
    block = 256
    for at in range(0, members.shape[0], block):
        member = members[at : at + block, :]
        folded = (member.astype(F32) * step_d).astype(BF16)
        offset = jnp.sum(
            lax.dot_general(parts, member, contract, preferred_element_type=F32),
            axis=0,
            keepdims=True,
        )
        top = jnp.max(
            lax.dot_general(own[...], folded, contract, preferred_element_type=F32),
            axis=0,
            keepdims=True,
        )
        top = jnp.maximum(
            top,
            jnp.max(
                lax.dot_general(other[...], folded, contract, preferred_element_type=F32),
                axis=0,
                keepdims=True,
            ),
        )
        best[:, at : at + block] = top + offset


def hidden_kernel(keys, own, other, w0, w1, w2, w3, hidden, weights, sems):
    chip, core = chip_and_core()
    rows = w0.shape[0] // 8
    copies = []
    for piece, chips in zip((w0, w1, w2, w3), keys):
        for slot, key in enumerate(chips):
            for half in range(2):
                device = (chip ^ key) * 2 + (core + half) % 2
                copies.append(
                    pltpu.make_async_copy(
                        piece.at[pl.ds((2 * slot + half) * rows, rows), :],
                        weights.at[pl.ds(pl.multiple_of(device * rows, rows), rows), :],
                        sems.at[len(copies)],
                    )
                )
    for copy in copies:
        copy.start()
    for copy in copies:
        copy.wait()
    count = own.shape[0]
    block = 256
    for at in range(0, 2 * count, block):
        features = own[at : at + block, :] if at < count else other[at - count : at - count + block, :]
        v = jnp.dot(features, weights[...], preferred_element_type=F32)
        v = 0.5 * v
        hidden[at : at + block, :] = (v * (1.0 + jnp.tanh(v))).astype(BF16)


def embed_kernel(keys, mine, theirs, w0, w1, w2, w3, own, other, bounds, weights, sems):
    chip, core = chip_and_core()
    rows = w0.shape[0] // 8
    copies = []
    for piece, chips in zip((w0, w1, w2, w3), keys):
        for slot, key in enumerate(chips):
            for half in range(2):
                device = (chip ^ key) * 2 + (core + half) % 2
                copies.append(
                    pltpu.make_async_copy(
                        piece.at[pl.ds((2 * slot + half) * rows, rows), :],
                        weights.at[pl.ds(pl.multiple_of(device * rows, rows), rows), :],
                        sems.at[len(copies)],
                    )
                )
    for copy in copies:
        copy.start()
    for copy in copies:
        copy.wait()
    count = own.shape[0]
    depth = mine.shape[1]
    here = pl.ds(pl.multiple_of(core * depth, depth), depth)
    there = pl.ds(pl.multiple_of((1 - core) * depth, depth), depth)
    block = 256
    upper = lower = None
    for at in range(0, 2 * count, block):
        flip = at + count if at < count else at - count
        e = jnp.dot(
            mine[at : at + block, :], weights[here, :], preferred_element_type=F32
        ) + jnp.dot(
            theirs[flip : flip + block, :], weights[there, :], preferred_element_type=F32
        )
        if at < count:
            own[at : at + block, :] = e
        else:
            other[at - count : at - count + block, :] = e
        top = jnp.max(e, axis=0, keepdims=True)
        bottom = jnp.min(e, axis=0, keepdims=True)
        upper = top if upper is None else jnp.maximum(upper, top)
        lower = bottom if lower is None else jnp.minimum(lower, bottom)
    bounds[0:1, :] = upper
    bounds[1:2, :] = -lower


def code_kernel(own, other, here, there, codes):
    _, core = chip_and_core()
    width = own.shape[1]
    for values, bounds, part in ((own, here, core), (other, there, 1 - core)):
        upper = bounds[0:1, :]
        lower = -bounds[1:2, :]
        mid = (upper + lower) * 0.5
        scale = 7.5 / ((upper - lower) * 0.5 + 1e-05)
        at = pl.ds(pl.multiple_of(part * width, width), width)
        codes[:, at] = ((values[...] - mid) * scale).astype(BF16)


def call(kernel, out, specs, scratch=(), limit=24):
    return pl.pallas_call(
        kernel,
        out_shape=out,
        in_specs=specs,
        out_specs=jax.tree.map(lambda _: VMEM, out),
        scratch_shapes=scratch,
        compiler_params=pltpu.CompilerParams(vmem_limit_bytes=limit * MIB),
    )


def shape(dims, dtype):
    return jax.ShapeDtypeStruct(dims, dtype)


def half_columns(x, core):
    width = x.shape[1] // 2
    return lax.dynamic_slice_in_dim(x, core * width, width, 1)


def by_permutes(n, n_rep, items, w_in, w_out, users, res_codes, range_idx, range_lo, range_step):
    move = lambda x, k: swap(x, "fsdp", n, k)
    _, core = chip_and_core()
    z_first = tuple(tuple(b + 4 * j for j in range(4)) for b in range(4))
    xy_first = tuple(tuple(4 * b + j for j in range(4)) for b in range(4))

    user_plane = jnp.concatenate(
        [users[0]] + [move(users[0], k) for k in (2, 4, 6)], axis=0
    )

    in_rows = jnp.concatenate(
        [half_columns(w_in, core), move(half_columns(w_in, 1 - core), 1)], axis=0
    )
    out_rows = jnp.concatenate(
        [half_columns(w_out, core), move(half_columns(w_out, 1 - core), 1)], axis=0
    )
    in_column = jnp.concatenate([in_rows] + [move(in_rows, k) for k in (8, 16, 24)], axis=0)
    in_pieces = [in_column] + [move(in_column, k) for k in (2, 4, 6)]
    out_column = jnp.concatenate([out_rows] + [move(out_rows, k) for k in (8, 16, 24)], axis=0)
    out_pieces = [out_column] + [move(out_column, k) for k in (2, 4, 6)]
    user_pieces = [user_plane] + [move(user_plane, k) for k in (8, 16, 24)]

    features = items[0]
    count, d_in = features.shape
    features_other = move(features, 1)
    codes = res_codes[0].astype(BF16)
    codes_other = move(codes, 1)

    members = n // 2 * users.shape[1]
    depth = users.shape[2]
    best = call(
        functools.partial(score_kernel, xy_first),
        shape((1, members), F32),
        [VMEM, SMEM, SMEM, VMEM, VMEM] + [ANY] * 4,
        [pltpu.VMEM((members, depth), BF16), pltpu.SemaphoreType.DMA((16,))],
    )(range_idx[None, :], range_lo, range_step, codes, codes_other, *user_pieces)

    wide = w_in.shape[1] // 2
    hidden = call(
        functools.partial(hidden_kernel, z_first),
        shape((2 * count, wide), BF16),
        [VMEM, VMEM] + [ANY] * 4,
        [pltpu.VMEM((d_in, wide), BF16), pltpu.SemaphoreType.DMA((32,))],
    )(features, features_other, *in_pieces)
    hidden_other = move(hidden, 1)

    width = w_out.shape[1] // 2
    own, other, bounds = call(
        functools.partial(embed_kernel, z_first),
        (
            shape((count, width), F32),
            shape((count, width), F32),
            shape((2, width), F32),
        ),
        [VMEM, VMEM] + [ANY] * 4,
        [pltpu.VMEM((2 * wide, width), BF16), pltpu.SemaphoreType.DMA((32,))],
    )(hidden, hidden_other, *out_pieces)
    received = move(other, 1)

    merged = jnp.concatenate([bounds, best], axis=0)
    for k in (2, 4, 8, 16):
        merged = jnp.maximum(merged, move(merged, k))
    bounds = merged[:2]
    if n_rep > 1:
        bounds = lax.pmax(bounds, "rep")
    new_codes = call(
        code_kernel,
        shape((count, 2 * width), BF16),
        [VMEM] * 4,
    )(own, received, bounds, move(bounds, 1))
    chip, _ = chip_and_core()
    each = users.shape[1]
    mine = lax.dynamic_slice_in_dim(merged[2:], chip * each, each, 1)
    return new_codes[None], mine


def on_any(items, w_in, w_out, users, res_codes, range_idx, range_lo, range_step):
    features = items[0]
    dot = functools.partial(jnp.dot, preferred_element_type=F32)
    first = dot(features, lax.all_gather(w_in, "fsdp", axis=0, tiled=True))
    hidden = jax.nn.silu(first).astype(BF16)
    embed = dot(hidden, lax.all_gather(w_out, "fsdp", axis=0, tiled=True))
    upper = lax.pmax(jnp.max(embed, axis=0), ("fsdp", "rep"))
    lower = lax.pmin(jnp.min(embed, axis=0), ("fsdp", "rep"))
    mid = (upper + lower) * 0.5
    half = (upper - lower) * 0.5
    new_codes = (7.5 * (embed - mid) / (half + 1e-05)).astype(BF16)[None]
    levels = jnp.arange(range_lo.shape[0], dtype=jnp.int32)
    match = (range_idx[None, :] == levels[:, None]).astype(F32)
    step_d = jnp.sum(range_step[:, None] * match, axis=0)
    lo_d = jnp.sum(range_lo[:, None] * match, axis=0)
    member = lax.all_gather(users, "fsdp", axis=1, tiled=True)[0]
    folded = (member.astype(F32) * step_d).astype(BF16)
    offset = jnp.dot(member.astype(F32), lo_d, precision=lax.Precision.HIGHEST)
    scores = dot(res_codes[0].astype(BF16), folded.T)
    merged = lax.pmax((jnp.max(scores, axis=0) + offset)[None], "fsdp")
    count = users.shape[1]
    best = lax.dynamic_slice_in_dim(merged, lax.axis_index("fsdp") * count, count, 1)
    return new_codes, best


def solution(mesh):
    n = mesh.shape["fsdp"]
    body = on_any
    if n == 32:
        body = functools.partial(by_permutes, n, mesh.shape["rep"])
    return jax.shard_map(
        body,
        mesh=mesh,
        in_specs=(
            P("rep", ("grp", "fsdp"), None),
            P("fsdp", None),
            P("fsdp", None),
            P("rep", ("grp", "fsdp"), None),
            P("rep", ("grp", "fsdp"), None),
            P("grp"),
            P("grp"),
            P("grp"),
        ),
        out_specs=(P("rep", ("grp", "fsdp"), None), P("rep", ("grp", "fsdp"))),
        check_vma=False,
    )
```

```python
import functools

import jax
import jax.numpy as jnp
from jax import lax
from jax.experimental import pallas as pl
from jax.experimental.pallas import tpu as pltpu
from jax.sharding import PartitionSpec as P

VMEM = pl.BlockSpec(memory_space=pltpu.VMEM)
SMEM = pl.BlockSpec(memory_space=pltpu.SMEM)
BF16 = jnp.bfloat16
F32 = jnp.float32
MIB = 1 << 20


def swap(x, axis, n, k):
    return lax.ppermute(x, axis, [(i, i ^ k) for i in range(n)])


def chip_and_core():
    me = lax.axis_index("fsdp")
    return me // 2, me % 2


def score_parts(idx, lo, step):
    index = idx[...]
    step_d = jnp.zeros(index.shape, F32)
    lo_d = jnp.zeros(index.shape, F32)
    for level in range(lo.shape[0]):
        step_d = jnp.where(index == level, step[level], step_d)
        lo_d = jnp.where(index == level, lo[level], lo_d)
    high = lo_d.astype(BF16)
    rest = lo_d - high.astype(F32)
    middle = rest.astype(BF16)
    low = rest - middle.astype(F32)
    row = lax.broadcasted_iota(jnp.int32, (16, index.shape[1]), 0)
    parts = jnp.where(
        row == 0,
        high.astype(F32),
        jnp.where(row == 1, middle.astype(F32), jnp.where(row == 2, low, 0.0)),
    ).astype(BF16)
    return step_d, parts


def score(step_d, parts, own, other, member):
    contract = (((1,), (1,)), ((), ()))
    product = lambda left, right: lax.dot_general(
        left, right, contract, preferred_element_type=F32
    )
    folded = (member.astype(F32) * step_d).astype(BF16)
    most = jnp.maximum(
        jnp.max(product(own[...], folded), axis=0, keepdims=True),
        jnp.max(product(other[...], folded), axis=0, keepdims=True),
    )
    return most + jnp.sum(product(parts, member), axis=0, keepdims=True)


def near_score_kernel(idx, lo, step, own, other, members, best):
    step_d, parts = score_parts(idx, lo, step)
    best[...] = score(step_d, parts, own, other, members[...])


def far_score_kernel(idx, lo, step, own, other, members, near, best):
    chip, _ = chip_and_core()
    step_d, parts = score_parts(idx, lo, step)
    found = jnp.concatenate(
        [near[...], score(step_d, parts, own, other, members[...])], axis=1
    )
    total = found.shape[1]
    each = total // 16
    lane = lax.broadcasted_iota(jnp.int32, found.shape, 1)
    for bit in (1, 2, 4, 8):
        far = bit * each
        crossed = jnp.where(
            (lane // far) % 2 == 1,
            pltpu.roll(found, far, 1),
            pltpu.roll(found, total - far, 1),
        )
        found = jnp.where((chip // bit) % 2 == 1, crossed, found)
    best[...] = found


def order_kernel(own, other, ordered):
    chip, core = chip_and_core()
    count, depth = own.shape
    each = depth // 32
    row = lax.broadcasted_iota(jnp.int32, (depth, depth), 0)
    col = lax.broadcasted_iota(jnp.int32, (depth, depth), 1)
    slot = col // each
    key = slot // 8 + 4 * ((slot // 2) % 4)
    source = ((chip ^ key) * 2 + (core + slot) % 2) * each + col % each
    pick = jnp.where(row == source, 1.0, 0.0).astype(BF16)
    for at, features in ((0, own), (count, other)):
        ordered[at : at + count, :] = jnp.dot(
            features[...], pick, preferred_element_type=F32
        ).astype(BF16)


def hidden_kernel(features, w0, w1, w2, w3, hidden):
    weights = jnp.concatenate([w[...] for w in (w0, w1, w2, w3)], axis=0)
    block = 256
    for at in range(0, features.shape[0], block):
        v = 0.5 * jnp.dot(
            features[at : at + block, :], weights, preferred_element_type=F32
        )
        hidden[at : at + block, :] = (v * (1.0 + jnp.tanh(v))).astype(BF16)


def add_up(keys, mine, theirs, pieces, finish):
    chip, core = chip_and_core()
    depth = mine.shape[1]
    rows = pieces[0].shape[0] // 4
    count = mine.shape[0]
    block = 256
    near = chip // 8 == core

    def work(first, second, first_is_mine):
        for at in range(0, count, block):
            flip = (at + count // 2) % count
            total = None
            for piece, chips in zip(pieces, keys):
                left = []
                for slot, key in enumerate(chips):
                    source = first if slot < 2 else second
                    start = at if (slot < 2) == first_is_mine else flip
                    column = pl.multiple_of((((chip ^ key) * rows) % depth), rows)
                    left.append(source[start : start + block, pl.ds(column, rows)])
                product = jnp.dot(
                    jnp.concatenate(left, axis=1), piece[...], preferred_element_type=F32
                )
                total = product if total is None else total + product
            finish(at, total)

    @pl.when(near)
    def _():
        work(mine, theirs, True)

    @pl.when(jnp.logical_not(near))
    def _():
        work(theirs, mine, False)


def first_embed_kernel(keys, mine, theirs, w0, w1, partial):
    def finish(at, total):
        partial[at : at + total.shape[0], :] = total

    add_up(keys, mine, theirs, (w0, w1), finish)


def last_embed_kernel(keys, mine, theirs, w0, w1, partial, own, other, bounds):
    count = own.shape[0]
    bounds[...] = jnp.full(bounds.shape, -jnp.inf, F32)

    def finish(at, total):
        total = total + partial[at : at + total.shape[0], :]
        if at < count:
            own[at : at + total.shape[0], :] = total
        else:
            other[at - count : at - count + total.shape[0], :] = total
        top = jnp.max(total, axis=0, keepdims=True)
        bottom = jnp.max(-total, axis=0, keepdims=True)
        bounds[0:1, :] = jnp.maximum(bounds[0:1, :], top)
        bounds[1:2, :] = jnp.maximum(bounds[1:2, :], bottom)

    add_up(keys, mine, theirs, (w0, w1), finish)


def code_kernel(own, other, here, there, codes):
    _, core = chip_and_core()
    width = own.shape[1]
    for values, bounds, part in ((own, here, core), (other, there, 1 - core)):
        upper = bounds[0:1, :]
        lower = -bounds[1:2, :]
        mid = (upper + lower) * 0.5
        scale = 7.5 / ((upper - lower) * 0.5 + 1e-05)
        at = pl.ds(pl.multiple_of(part * width, width), width)
        codes[:, at] = ((values[...] - mid) * scale).astype(BF16)


def call(kernel, out, specs, flops, limit=24):
    outs = jax.tree.leaves(out)
    return pl.pallas_call(
        kernel,
        out_shape=out,
        in_specs=specs,
        out_specs=jax.tree.map(lambda _: VMEM, out),
        compiler_params=pltpu.CompilerParams(vmem_limit_bytes=limit * MIB),
        cost_estimate=pl.CostEstimate(
            flops=flops,
            transcendentals=0,
            bytes_accessed=sum(o.size * o.dtype.itemsize for o in outs),
        ),
    )


def shape(dims, dtype):
    return jax.ShapeDtypeStruct(dims, dtype)


def half_columns(x, core):
    width = x.shape[1] // 2
    return lax.dynamic_slice_in_dim(x, core * width, width, 1)


def by_permutes(n, n_rep, items, w_in, w_out, users, res_codes, range_idx, range_lo, range_step):
    move = lambda x, k: swap(x, "fsdp", n, k)
    cat = lambda *parts: jnp.concatenate(parts, axis=0)
    chip, core = chip_and_core()
    keys = tuple(tuple(b + 4 * j for j in range(4)) for b in range(4))
    count, d_in = items.shape[1:]
    wide = w_in.shape[1] // 2
    width = w_out.shape[1] // 2

    in_rows = cat(half_columns(w_in, core), move(half_columns(w_in, 1 - core), 1))
    in_column = cat(in_rows, *(move(in_rows, k) for k in (8, 16, 24)))
    here, there = half_columns(w_out, core), move(half_columns(w_out, 1 - core), 1)
    out_rows = jnp.where(core == 0, cat(here, there), cat(there, here))
    out_pair = cat(out_rows, move(out_rows, 8))
    user_pair = cat(users[0], move(users[0], 2))
    user_plane = cat(user_pair, move(user_pair, 4))

    features = items[0]
    ordered = call(
        order_kernel, shape((2 * count, d_in), BF16), [VMEM, VMEM], 4 * count * d_in * d_in
    )(features, move(features, 1))
    in_column, out_pair, user_plane, ordered, resident = lax.optimization_barrier(
        (in_column, out_pair, user_plane, ordered, res_codes[0])
    )
    in_pieces = [in_column] + [move(in_column, k) for k in (2, 4, 6)]
    out_column = cat(out_pair, move(out_pair, 16))
    near_users = cat(user_plane, move(user_plane, 8))
    codes = resident.astype(BF16)
    codes_other = move(codes, 1)

    *in_pieces, out_column, near_users = lax.optimization_barrier(
        (*in_pieces, out_column, near_users)
    )
    out_pieces = [out_column] + [move(out_column, k) for k in (2, 4, 6)]
    far_users = move(near_users, 16)
    last_pieces, far_users = lax.optimization_barrier((out_pieces[2:], far_users))
    ranges = (range_idx[None, :], range_lo, range_step)
    members = near_users.shape[0]
    score_flops = 4 * members * count * users.shape[2]
    near_best = call(
        near_score_kernel,
        shape((1, members), F32),
        [VMEM, SMEM, SMEM] + [VMEM] * 3,
        score_flops,
    )(*ranges, codes, codes_other, near_users)

    hidden = call(
        hidden_kernel,
        shape((2 * count, wide), BF16),
        [VMEM] * 5,
        4 * count * d_in * wide,
    )(ordered, *in_pieces)
    hidden_other = move(hidden, 1)

    best = call(
        far_score_kernel,
        shape((1, 2 * members), F32),
        [VMEM, SMEM, SMEM] + [VMEM] * 4,
        score_flops,
    )(*ranges, codes, codes_other, far_users, near_best)

    partial = call(
        functools.partial(first_embed_kernel, keys[:2]),
        shape((2 * count, width), F32),
        [VMEM] * 4,
        4 * count * wide * width,
    )(hidden, hidden_other, *out_pieces[:2])
    own, other, bounds = call(
        functools.partial(last_embed_kernel, keys[2:]),
        (
            shape((count, width), F32),
            shape((count, width), F32),
            shape((2, width), F32),
        ),
        [VMEM] * 5,
        4 * count * wide * width,
    )(hidden, hidden_other, *last_pieces, partial)
    received = move(other, 1)

    merged = cat(bounds, best)
    for k in (2, 4, 8, 16):
        merged = jnp.maximum(merged, move(merged, k))
    bounds = merged[:2]
    if n_rep > 1:
        bounds = lax.pmax(bounds, "rep")
    new_codes = call(
        code_kernel, shape((count, 2 * width), BF16), [VMEM] * 4, 4 * count * width
    )(own, received, bounds, move(bounds, 1))
    each = users.shape[1]
    mine = lax.dynamic_slice_in_dim(merged[2:], chip * each, each, 1)
    return new_codes[None], mine


def on_any(items, w_in, w_out, users, res_codes, range_idx, range_lo, range_step):
    features = items[0]
    dot = functools.partial(jnp.dot, preferred_element_type=F32)
    first = dot(features, lax.all_gather(w_in, "fsdp", axis=0, tiled=True))
    hidden = jax.nn.silu(first).astype(BF16)
    embed = dot(hidden, lax.all_gather(w_out, "fsdp", axis=0, tiled=True))
    upper = lax.pmax(jnp.max(embed, axis=0), ("fsdp", "rep"))
    lower = lax.pmin(jnp.min(embed, axis=0), ("fsdp", "rep"))
    mid = (upper + lower) * 0.5
    half = (upper - lower) * 0.5
    new_codes = (7.5 * (embed - mid) / (half + 1e-05)).astype(BF16)[None]
    levels = jnp.arange(range_lo.shape[0], dtype=jnp.int32)
    match = (range_idx[None, :] == levels[:, None]).astype(F32)
    step_d = jnp.sum(range_step[:, None] * match, axis=0)
    lo_d = jnp.sum(range_lo[:, None] * match, axis=0)
    member = lax.all_gather(users, "fsdp", axis=1, tiled=True)[0]
    folded = (member.astype(F32) * step_d).astype(BF16)
    offset = jnp.dot(member.astype(F32), lo_d, precision=lax.Precision.HIGHEST)
    scores = dot(res_codes[0].astype(BF16), folded.T)
    merged = lax.pmax((jnp.max(scores, axis=0) + offset)[None], "fsdp")
    count = users.shape[1]
    best = lax.dynamic_slice_in_dim(merged, lax.axis_index("fsdp") * count, count, 1)
    return new_codes, best


def solution(mesh):
    n = mesh.shape["fsdp"]
    body = on_any
    if n == 32:
        body = functools.partial(by_permutes, n, mesh.shape["rep"])
    return jax.shard_map(
        body,
        mesh=mesh,
        in_specs=(
            P("rep", ("grp", "fsdp"), None),
            P("fsdp", None),
            P("fsdp", None),
            P("rep", ("grp", "fsdp"), None),
            P("rep", ("grp", "fsdp"), None),
            P("grp"),
            P("grp"),
            P("grp"),
        ),
        out_specs=(P("rep", ("grp", "fsdp"), None), P("rep", ("grp", "fsdp"))),
        check_vma=False,
    )
```

```python
import functools

import jax
import jax.numpy as jnp
from jax import lax
from jax.experimental import pallas as pl
from jax.experimental.pallas import tpu as pltpu
from jax.sharding import PartitionSpec as P

VMEM = pl.BlockSpec(memory_space=pltpu.VMEM)
SMEM = pl.BlockSpec(memory_space=pltpu.SMEM)
BF16 = jnp.bfloat16
F32 = jnp.float32
MIB = 1 << 20


def swap(x, axis, n, k):
    return lax.ppermute(x, axis, [(i, i ^ k) for i in range(n)])


def chip_and_core():
    me = lax.axis_index("fsdp")
    return me // 2, me % 2


def score_parts(idx, lo, step):
    index = idx[...]
    step_d = jnp.zeros(index.shape, F32)
    lo_d = jnp.zeros(index.shape, F32)
    for level in range(lo.shape[0]):
        step_d = jnp.where(index == level, step[level], step_d)
        lo_d = jnp.where(index == level, lo[level], lo_d)
    high = lo_d.astype(BF16)
    rest = lo_d - high.astype(F32)
    middle = rest.astype(BF16)
    low = rest - middle.astype(F32)
    row = lax.broadcasted_iota(jnp.int32, (16, index.shape[1]), 0)
    parts = jnp.where(
        row == 0,
        high.astype(F32),
        jnp.where(row == 1, middle.astype(F32), jnp.where(row == 2, low, 0.0)),
    ).astype(BF16)
    return step_d, parts


def score(step_d, parts, own, other, member):
    contract = (((1,), (1,)), ((), ()))
    product = lambda left, right: lax.dot_general(
        left, right, contract, preferred_element_type=F32
    )
    folded = (member.astype(F32) * step_d).astype(BF16)
    most = jnp.maximum(
        jnp.max(product(own[...], folded), axis=0, keepdims=True),
        jnp.max(product(other[...], folded), axis=0, keepdims=True),
    )
    return most + jnp.sum(product(parts, member), axis=0, keepdims=True)


def near_score_kernel(idx, lo, step, own, other, u0, u1, best):
    step_d, parts = score_parts(idx, lo, step)
    members = jnp.concatenate([u0[...], u1[...]], axis=0)
    best[...] = score(step_d, parts, own, other, members)


def far_score_kernel(idx, lo, step, own, other, u0, u1, near, best):
    chip, _ = chip_and_core()
    step_d, parts = score_parts(idx, lo, step)
    members = jnp.concatenate([u0[...], u1[...]], axis=0)
    found = jnp.concatenate(
        [near[...], score(step_d, parts, own, other, members)], axis=1
    )
    total = found.shape[1]
    each = total // 16
    lane = lax.broadcasted_iota(jnp.int32, found.shape, 1)
    for bit in (1, 2, 4, 8):
        far = bit * each
        crossed = jnp.where(
            (lane // far) % 2 == 1,
            pltpu.roll(found, far, 1),
            pltpu.roll(found, total - far, 1),
        )
        found = jnp.where((chip // bit) % 2 == 1, crossed, found)
    best[...] = found


def order_kernel(own, other, ordered):
    chip, core = chip_and_core()
    count, depth = own.shape
    each = depth // 32
    row = lax.broadcasted_iota(jnp.int32, (depth, depth), 0)
    col = lax.broadcasted_iota(jnp.int32, (depth, depth), 1)
    slot = col // each
    key = slot // 8 + 4 * ((slot // 2) % 4)
    source = ((chip ^ key) * 2 + (core + slot) % 2) * each + col % each
    pick = jnp.where(row == source, 1.0, 0.0).astype(BF16)
    for at, features in ((0, own), (count, other)):
        ordered[at : at + count, :] = jnp.dot(
            features[...], pick, preferred_element_type=F32
        ).astype(BF16)


def hidden_kernel(features, w0, w1, w2, w3, hidden):
    weights = jnp.concatenate([w[...] for w in (w0, w1, w2, w3)], axis=0)
    block = 256
    for at in range(0, features.shape[0], block):
        v = 0.5 * jnp.dot(
            features[at : at + block, :], weights, preferred_element_type=F32
        )
        hidden[at : at + block, :] = (v * (1.0 + jnp.tanh(v))).astype(BF16)


def add_up(keys, mine, theirs, pieces, finish):
    chip, core = chip_and_core()
    depth = mine.shape[1]
    rows = pieces[0].shape[0] // len(keys[0])
    count = mine.shape[0]
    block = 256
    near = chip // 8 == core

    def work(first, second, first_is_mine):
        for at in range(0, count, block):
            flip = (at + count // 2) % count
            total = None
            for piece, chips in zip(pieces, keys):
                left = []
                for key in chips:
                    source = first if key < 8 else second
                    start = at if (key < 8) == first_is_mine else flip
                    column = pl.multiple_of((((chip ^ key) * rows) % depth), rows)
                    left.append(source[start : start + block, pl.ds(column, rows)])
                product = jnp.dot(
                    jnp.concatenate(left, axis=1), piece[...], preferred_element_type=F32
                )
                total = product if total is None else total + product
            finish(at, total)

    @pl.when(near)
    def _():
        work(mine, theirs, True)

    @pl.when(jnp.logical_not(near))
    def _():
        work(theirs, mine, False)


def first_embed_kernel(keys, mine, theirs, *refs):
    *pieces, partial = refs

    def finish(at, total):
        partial[at : at + total.shape[0], :] = total

    add_up(keys, mine, theirs, pieces, finish)


def last_embed_kernel(keys, mine, theirs, *refs):
    *pieces, partial, best, own, other, bounds = refs
    count = own.shape[0]
    bounds[...] = jnp.full(bounds.shape, -jnp.inf, F32)
    bounds[2:3, :] = best[...]

    def finish(at, total):
        total = total + partial[at : at + total.shape[0], :]
        if at < count:
            own[at : at + total.shape[0], :] = total
        else:
            other[at - count : at - count + total.shape[0], :] = total
        top = jnp.max(total, axis=0, keepdims=True)
        bottom = jnp.max(-total, axis=0, keepdims=True)
        bounds[0:1, :] = jnp.maximum(bounds[0:1, :], top)
        bounds[1:2, :] = jnp.maximum(bounds[1:2, :], bottom)

    add_up(keys, mine, theirs, pieces, finish)


def code_kernel(own, other, here, there, codes):
    _, core = chip_and_core()
    width = own.shape[1]
    for values, bounds, part in ((own, here, core), (other, there, 1 - core)):
        upper = bounds[0:1, :]
        lower = -bounds[1:2, :]
        mid = (upper + lower) * 0.5
        scale = 7.5 / ((upper - lower) * 0.5 + 1e-05)
        at = pl.ds(pl.multiple_of(part * width, width), width)
        codes[:, at] = ((values[...] - mid) * scale).astype(BF16)


def call(kernel, out, specs, flops, limit=24):
    outs = jax.tree.leaves(out)
    return pl.pallas_call(
        kernel,
        out_shape=out,
        in_specs=specs,
        out_specs=jax.tree.map(lambda _: VMEM, out),
        compiler_params=pltpu.CompilerParams(vmem_limit_bytes=limit * MIB),
        cost_estimate=pl.CostEstimate(
            flops=flops,
            transcendentals=0,
            bytes_accessed=sum(o.size * o.dtype.itemsize for o in outs),
        ),
    )


def shape(dims, dtype):
    return jax.ShapeDtypeStruct(dims, dtype)


def half_columns(x, core):
    width = x.shape[1] // 2
    return lax.dynamic_slice_in_dim(x, core * width, width, 1)


def by_permutes(n, n_rep, items, w_in, w_out, users, res_codes, range_idx, range_lo, range_step):
    move = lambda x, k: swap(x, "fsdp", n, k)
    cat = lambda *parts: jnp.concatenate(parts, axis=0)
    chip, core = chip_and_core()
    keys = tuple(tuple(b + 4 * j for j in range(4)) for b in range(4))
    count, d_in = items.shape[1:]
    wide = w_in.shape[1] // 2
    width = w_out.shape[1] // 2

    in_rows = cat(half_columns(w_in, core), move(half_columns(w_in, 1 - core), 1))
    in_column = cat(in_rows, *(move(in_rows, k) for k in (8, 16, 24)))
    here, there = half_columns(w_out, core), move(half_columns(w_out, 1 - core), 1)
    out_rows = jnp.where(core == 0, cat(here, there), cat(there, here))
    user_pair = cat(users[0], move(users[0], 2))
    user_plane = cat(user_pair, move(user_pair, 4))
    features = items[0]
    ordered = call(
        order_kernel, shape((2 * count, d_in), BF16), [VMEM, VMEM], 4 * count * d_in * d_in
    )(features, move(features, 1))
    in_column, out_rows, user_plane, ordered, resident = lax.optimization_barrier(
        (in_column, out_rows, user_plane, ordered, res_codes[0])
    )

    in_pieces = [in_column] + [move(in_column, k) for k in (2, 4, 6)]
    out_far = move(out_rows, 16)
    out_column = cat(out_rows, move(out_rows, 8), out_far, move(out_far, 8))
    codes = resident.astype(BF16)
    codes_other = move(codes, 1)
    *in_pieces, out_column, user_plane = lax.optimization_barrier(
        (*in_pieces, out_column, user_plane)
    )

    hidden = call(
        hidden_kernel,
        shape((2 * count, wide), BF16),
        [VMEM] * 5,
        4 * count * d_in * wide,
    )(ordered, *in_pieces)
    out_x, out_y = move(out_column, 2), move(out_column, 4)
    user_near, user_far = move(user_plane, 8), move(user_plane, 16)
    out_x, out_y, user_near, user_far, hidden = lax.optimization_barrier(
        (out_x, out_y, user_near, user_far, hidden)
    )
    half = out_column.shape[0] // 2
    out_low, out_high = move(out_y[:half], 2), move(out_x[half:], 4)
    user_last = move(user_far, 8)

    ranges = (range_idx[None, :], range_lo, range_step)
    members = 2 * user_plane.shape[0]
    score_flops = 4 * members * count * users.shape[2]
    near_best = call(
        near_score_kernel,
        shape((1, members), F32),
        [VMEM, SMEM, SMEM] + [VMEM] * 4,
        score_flops,
    )(*ranges, codes, codes_other, user_plane, user_near)
    hidden_other = move(hidden, 1)
    best = call(
        far_score_kernel,
        shape((1, 2 * members), F32),
        [VMEM, SMEM, SMEM] + [VMEM] * 5,
        score_flops,
    )(*ranges, codes, codes_other, user_far, user_last, near_best)

    partial = call(
        functools.partial(first_embed_kernel, keys[:3]),
        shape((2 * count, width), F32),
        [VMEM] * 5,
        6 * count * wide * width,
    )(hidden, hidden_other, out_column, out_x, out_y)
    own, other, merged = call(
        functools.partial(last_embed_kernel, (keys[3][:2], keys[3][2:])),
        (
            shape((count, width), F32),
            shape((count, width), F32),
            shape((3, width), F32),
        ),
        [VMEM] * 6,
        2 * count * wide * width,
    )(hidden, hidden_other, out_low, out_high, partial, best)
    received = move(other, 1)

    for k in (2, 4, 8, 16):
        merged = jnp.maximum(merged, move(merged, k))
    bounds = merged[:2]
    if n_rep > 1:
        bounds = lax.pmax(bounds, "rep")
    new_codes = call(
        code_kernel, shape((count, 2 * width), BF16), [VMEM] * 4, 4 * count * width
    )(own, received, bounds, move(bounds, 1))
    each = users.shape[1]
    mine = lax.dynamic_slice_in_dim(merged[2:], chip * each, each, 1)
    return new_codes[None], mine


def on_any(items, w_in, w_out, users, res_codes, range_idx, range_lo, range_step):
    features = items[0]
    dot = functools.partial(jnp.dot, preferred_element_type=F32)
    first = dot(features, lax.all_gather(w_in, "fsdp", axis=0, tiled=True))
    hidden = jax.nn.silu(first).astype(BF16)
    embed = dot(hidden, lax.all_gather(w_out, "fsdp", axis=0, tiled=True))
    upper = lax.pmax(jnp.max(embed, axis=0), ("fsdp", "rep"))
    lower = lax.pmin(jnp.min(embed, axis=0), ("fsdp", "rep"))
    mid = (upper + lower) * 0.5
    half = (upper - lower) * 0.5
    new_codes = (7.5 * (embed - mid) / (half + 1e-05)).astype(BF16)[None]
    levels = jnp.arange(range_lo.shape[0], dtype=jnp.int32)
    match = (range_idx[None, :] == levels[:, None]).astype(F32)
    step_d = jnp.sum(range_step[:, None] * match, axis=0)
    lo_d = jnp.sum(range_lo[:, None] * match, axis=0)
    member = lax.all_gather(users, "fsdp", axis=1, tiled=True)[0]
    folded = (member.astype(F32) * step_d).astype(BF16)
    offset = jnp.dot(member.astype(F32), lo_d, precision=lax.Precision.HIGHEST)
    scores = dot(res_codes[0].astype(BF16), folded.T)
    merged = lax.pmax((jnp.max(scores, axis=0) + offset)[None], "fsdp")
    count = users.shape[1]
    best = lax.dynamic_slice_in_dim(merged, lax.axis_index("fsdp") * count, count, 1)
    return new_codes, best


def solution(mesh):
    n = mesh.shape["fsdp"]
    body = on_any
    if n == 32:
        body = functools.partial(by_permutes, n, mesh.shape["rep"])
    return jax.shard_map(
        body,
        mesh=mesh,
        in_specs=(
            P("rep", ("grp", "fsdp"), None),
            P("fsdp", None),
            P("fsdp", None),
            P("rep", ("grp", "fsdp"), None),
            P("rep", ("grp", "fsdp"), None),
            P("grp"),
            P("grp"),
            P("grp"),
        ),
        out_specs=(P("rep", ("grp", "fsdp"), None), P("rep", ("grp", "fsdp"))),
        check_vma=False,
    )
```

```python
import functools

import jax
import jax.numpy as jnp
from jax import lax
from jax.experimental import pallas as pl
from jax.experimental.pallas import tpu as pltpu
from jax.sharding import PartitionSpec as P

VMEM = pl.BlockSpec(memory_space=pltpu.VMEM)
SMEM = pl.BlockSpec(memory_space=pltpu.SMEM)
BF16 = jnp.bfloat16
F32 = jnp.float32
MIB = 1 << 20


def swap(x, axis, n, k):
    return lax.ppermute(x, axis, [(i, i ^ k) for i in range(n)])


def chip_and_core():
    me = lax.axis_index("fsdp")
    return me // 2, me % 2


def score_parts(idx, lo, step):
    index = idx[...]
    step_d = jnp.zeros(index.shape, F32)
    lo_d = jnp.zeros(index.shape, F32)
    for level in range(lo.shape[0]):
        step_d = jnp.where(index == level, step[level], step_d)
        lo_d = jnp.where(index == level, lo[level], lo_d)
    high = lo_d.astype(BF16)
    rest = lo_d - high.astype(F32)
    middle = rest.astype(BF16)
    low = rest - middle.astype(F32)
    row = lax.broadcasted_iota(jnp.int32, (16, index.shape[1]), 0)
    parts = jnp.where(
        row == 0,
        high.astype(F32),
        jnp.where(row == 1, middle.astype(F32), jnp.where(row == 2, low, 0.0)),
    ).astype(BF16)
    return step_d, parts


def score(step_d, parts, own, other, member):
    contract = (((1,), (1,)), ((), ()))
    product = lambda left, right: lax.dot_general(
        left, right, contract, preferred_element_type=F32
    )
    folded = (member.astype(F32) * step_d).astype(BF16)
    most = jnp.maximum(
        jnp.max(product(own[...], folded), axis=0, keepdims=True),
        jnp.max(product(other[...], folded), axis=0, keepdims=True),
    )
    return most + jnp.sum(product(parts, member), axis=0, keepdims=True)


def near_score_kernel(idx, lo, step, own, other, u0, u1, best):
    step_d, parts = score_parts(idx, lo, step)
    members = jnp.concatenate([u0[...], u1[...]], axis=0)
    best[...] = score(step_d, parts, own, other, members)


def far_score_kernel(idx, lo, step, own, other, u0, u1, near, best):
    chip, _ = chip_and_core()
    step_d, parts = score_parts(idx, lo, step)
    members = jnp.concatenate([u0[...], u1[...]], axis=0)
    found = jnp.concatenate(
        [near[...], score(step_d, parts, own, other, members)], axis=1
    )
    total = found.shape[1]
    each = total // 16
    lane = lax.broadcasted_iota(jnp.int32, found.shape, 1)
    for bit in (1, 2, 4, 8):
        far = bit * each
        crossed = jnp.where(
            (lane // far) % 2 == 1,
            pltpu.roll(found, far, 1),
            pltpu.roll(found, total - far, 1),
        )
        found = jnp.where((chip // bit) % 2 == 1, crossed, found)
    best[...] = found


def order_kernel(own, other, ordered):
    chip, core = chip_and_core()
    count, depth = own.shape
    each = depth // 32
    row = lax.broadcasted_iota(jnp.int32, (depth, depth), 0)
    col = lax.broadcasted_iota(jnp.int32, (depth, depth), 1)
    slot = col // each
    key = slot // 8 + 4 * ((slot // 2) % 4)
    source = ((chip ^ key) * 2 + (core + slot) % 2) * each + col % each
    pick = jnp.where(row == source, 1.0, 0.0).astype(BF16)
    for at, features in ((0, own), (count, other)):
        ordered[at : at + count, :] = jnp.dot(
            features[...], pick, preferred_element_type=F32
        ).astype(BF16)


def hidden_kernel(features, w0, w1, w2, w3, hidden):
    weights = jnp.concatenate([w[...] for w in (w0, w1, w2, w3)], axis=0)
    block = 256
    for at in range(0, features.shape[0], block):
        v = 0.5 * jnp.dot(
            features[at : at + block, :], weights, preferred_element_type=F32
        )
        hidden[at : at + block, :] = (v * (1.0 + jnp.tanh(v))).astype(BF16)


def add_up(keys, mine, theirs, pieces, finish):
    chip, core = chip_and_core()
    depth = mine.shape[1]
    rows = pieces[0].shape[0] // len(keys[0])
    count = mine.shape[0]
    block = 256
    near = chip // 8 == core

    def work(first, second, first_is_mine):
        for at in range(0, count, block):
            flip = (at + count // 2) % count
            total = None
            for piece, chips in zip(pieces, keys):
                left = []
                for key in chips:
                    source = first if key < 8 else second
                    start = at if (key < 8) == first_is_mine else flip
                    column = pl.multiple_of((((chip ^ key) * rows) % depth), rows)
                    left.append(source[start : start + block, pl.ds(column, rows)])
                product = jnp.dot(
                    jnp.concatenate(left, axis=1), piece[...], preferred_element_type=F32
                )
                total = product if total is None else total + product
            finish(at, total)

    @pl.when(near)
    def _():
        work(mine, theirs, True)

    @pl.when(jnp.logical_not(near))
    def _():
        work(theirs, mine, False)


def first_embed_kernel(keys, mine, theirs, *refs):
    *pieces, partial = refs

    def finish(at, total):
        partial[at : at + total.shape[0], :] = total

    add_up(keys, mine, theirs, pieces, finish)


def last_embed_kernel(keys, mine, theirs, *refs):
    *pieces, partial, best, own, other, bounds = refs
    count = own.shape[0]
    bounds[...] = jnp.full(bounds.shape, -jnp.inf, F32)
    bounds[2:3, :] = best[...]

    def finish(at, total):
        total = total + partial[at : at + total.shape[0], :]
        if at < count:
            own[at : at + total.shape[0], :] = total
        else:
            other[at - count : at - count + total.shape[0], :] = total
        top = jnp.max(total, axis=0, keepdims=True)
        bottom = jnp.max(-total, axis=0, keepdims=True)
        bounds[0:1, :] = jnp.maximum(bounds[0:1, :], top)
        bounds[1:2, :] = jnp.maximum(bounds[1:2, :], bottom)

    add_up(keys, mine, theirs, pieces, finish)


def code_kernel(own, other, here, there, codes):
    _, core = chip_and_core()
    width = own.shape[1]
    for values, bounds, part in ((own, here, core), (other, there, 1 - core)):
        upper = bounds[0:1, :]
        lower = -bounds[1:2, :]
        mid = (upper + lower) * 0.5
        scale = 7.5 / ((upper - lower) * 0.5 + 1e-05)
        at = pl.ds(pl.multiple_of(part * width, width), width)
        codes[:, at] = ((values[...] - mid) * scale).astype(BF16)


def call(kernel, out, specs, flops, limit=24):
    outs = jax.tree.leaves(out)
    return pl.pallas_call(
        kernel,
        out_shape=out,
        in_specs=specs,
        out_specs=jax.tree.map(lambda _: VMEM, out),
        compiler_params=pltpu.CompilerParams(vmem_limit_bytes=limit * MIB),
        cost_estimate=pl.CostEstimate(
            flops=flops,
            transcendentals=0,
            bytes_accessed=sum(o.size * o.dtype.itemsize for o in outs),
        ),
    )


def shape(dims, dtype):
    return jax.ShapeDtypeStruct(dims, dtype)


def half_columns(x, core):
    width = x.shape[1] // 2
    return lax.dynamic_slice_in_dim(x, core * width, width, 1)


def most(x, others):
    for other in others:
        x = jnp.maximum(x, other)
    return x


def by_permutes(n, n_rep, items, w_in, w_out, users, res_codes, range_idx, range_lo, range_step):
    move = lambda x, k: swap(x, "fsdp", n, k)
    cat = lambda *parts: jnp.concatenate(parts, axis=0)
    chip, core = chip_and_core()
    keys = tuple(tuple(b + 4 * j for j in range(4)) for b in range(4))
    count, d_in = items.shape[1:]
    wide = w_in.shape[1] // 2
    width = w_out.shape[1] // 2

    in_rows = cat(half_columns(w_in, core), move(half_columns(w_in, 1 - core), 1))
    in_column = cat(in_rows, *(move(in_rows, k) for k in (8, 16, 24)))
    here, there = half_columns(w_out, core), move(half_columns(w_out, 1 - core), 1)
    out_rows = jnp.where(core == 0, cat(here, there), cat(there, here))
    user_pair = cat(users[0], move(users[0], 2))
    user_plane = cat(user_pair, move(user_pair, 4))
    features = items[0]
    ordered = call(
        order_kernel, shape((2 * count, d_in), BF16), [VMEM, VMEM], 4 * count * d_in * d_in
    )(features, move(features, 1))
    in_column, out_rows, user_plane, ordered, resident = lax.optimization_barrier(
        (in_column, out_rows, user_plane, ordered, res_codes[0])
    )

    in_pieces = [in_column] + [move(in_column, k) for k in (2, 4, 6)]
    out_far = move(out_rows, 16)
    out_column = cat(out_rows, move(out_rows, 8), out_far, move(out_far, 8))
    codes = resident.astype(BF16)
    codes_other = move(codes, 1)
    *in_pieces, out_column, user_plane = lax.optimization_barrier(
        (*in_pieces, out_column, user_plane)
    )

    hidden = call(
        hidden_kernel,
        shape((2 * count, wide), BF16),
        [VMEM] * 5,
        4 * count * d_in * wide,
    )(ordered, *in_pieces)
    out_x, out_y = move(out_column, 2), move(out_column, 4)
    user_near, user_far = move(user_plane, 8), move(user_plane, 16)
    out_x, out_y, user_near, user_far, hidden = lax.optimization_barrier(
        (out_x, out_y, user_near, user_far, hidden)
    )
    half = out_column.shape[0] // 2
    out_low, out_high = move(out_y[:half], 2), move(out_x[half:], 4)
    user_last = move(user_far, 8)

    ranges = (range_idx[None, :], range_lo, range_step)
    members = 2 * user_plane.shape[0]
    score_flops = 4 * members * count * users.shape[2]
    near_best = call(
        near_score_kernel,
        shape((1, members), F32),
        [VMEM, SMEM, SMEM] + [VMEM] * 4,
        score_flops,
    )(*ranges, codes, codes_other, user_plane, user_near)
    hidden_other = move(hidden, 1)
    partial = call(
        functools.partial(first_embed_kernel, keys[:3]),
        shape((2 * count, width), F32),
        [VMEM] * 5,
        6 * count * wide * width,
    )(hidden, hidden_other, out_column, out_x, out_y)
    near_best, partial = lax.optimization_barrier((near_best, partial))
    best = call(
        far_score_kernel,
        shape((1, 2 * members), F32),
        [VMEM, SMEM, SMEM] + [VMEM] * 5,
        score_flops,
    )(*ranges, codes, codes_other, user_far, user_last, near_best)

    own, other, merged = call(
        functools.partial(last_embed_kernel, (keys[3][:2], keys[3][2:])),
        (
            shape((count, width), F32),
            shape((count, width), F32),
            shape((3, width), F32),
        ),
        [VMEM] * 6,
        2 * count * wide * width,
    )(hidden, hidden_other, out_low, out_high, partial, best)
    received = move(other, 1)

    for keys in ((8, 16, 24), (2, 4, 6)):
        merged = most(merged, [move(merged, k) for k in keys])
    bounds = merged[:2]
    if n_rep > 1:
        bounds = lax.pmax(bounds, "rep")
    new_codes = call(
        code_kernel, shape((count, 2 * width), BF16), [VMEM] * 4, 4 * count * width
    )(own, received, bounds, move(bounds, 1))
    each = users.shape[1]
    mine = lax.dynamic_slice_in_dim(merged[2:], chip * each, each, 1)
    return new_codes[None], mine


def on_any(items, w_in, w_out, users, res_codes, range_idx, range_lo, range_step):
    features = items[0]
    dot = functools.partial(jnp.dot, preferred_element_type=F32)
    first = dot(features, lax.all_gather(w_in, "fsdp", axis=0, tiled=True))
    hidden = jax.nn.silu(first).astype(BF16)
    embed = dot(hidden, lax.all_gather(w_out, "fsdp", axis=0, tiled=True))
    upper = lax.pmax(jnp.max(embed, axis=0), ("fsdp", "rep"))
    lower = lax.pmin(jnp.min(embed, axis=0), ("fsdp", "rep"))
    mid = (upper + lower) * 0.5
    half = (upper - lower) * 0.5
    new_codes = (7.5 * (embed - mid) / (half + 1e-05)).astype(BF16)[None]
    levels = jnp.arange(range_lo.shape[0], dtype=jnp.int32)
    match = (range_idx[None, :] == levels[:, None]).astype(F32)
    step_d = jnp.sum(range_step[:, None] * match, axis=0)
    lo_d = jnp.sum(range_lo[:, None] * match, axis=0)
    member = lax.all_gather(users, "fsdp", axis=1, tiled=True)[0]
    folded = (member.astype(F32) * step_d).astype(BF16)
    offset = jnp.dot(member.astype(F32), lo_d, precision=lax.Precision.HIGHEST)
    scores = dot(res_codes[0].astype(BF16), folded.T)
    merged = lax.pmax((jnp.max(scores, axis=0) + offset)[None], "fsdp")
    count = users.shape[1]
    best = lax.dynamic_slice_in_dim(merged, lax.axis_index("fsdp") * count, count, 1)
    return new_codes, best


def solution(mesh):
    n = mesh.shape["fsdp"]
    body = on_any
    if n == 32:
        body = functools.partial(by_permutes, n, mesh.shape["rep"])
    return jax.shard_map(
        body,
        mesh=mesh,
        in_specs=(
            P("rep", ("grp", "fsdp"), None),
            P("fsdp", None),
            P("fsdp", None),
            P("rep", ("grp", "fsdp"), None),
            P("rep", ("grp", "fsdp"), None),
            P("grp"),
            P("grp"),
            P("grp"),
        ),
        out_specs=(P("rep", ("grp", "fsdp"), None), P("rep", ("grp", "fsdp"))),
        check_vma=False,
    )
```

```python
import functools

import jax
import jax.numpy as jnp
from jax import lax
from jax.experimental import pallas as pl
from jax.experimental.pallas import tpu as pltpu
from jax.sharding import PartitionSpec as P

VMEM = pl.BlockSpec(memory_space=pltpu.VMEM)
SMEM = pl.BlockSpec(memory_space=pltpu.SMEM)
BF16 = jnp.bfloat16
F32 = jnp.float32
MIB = 1 << 20


def swap(x, axis, n, k):
    return lax.ppermute(x, axis, [(i, i ^ k) for i in range(n)])


def chip_and_core():
    me = lax.axis_index("fsdp")
    return me // 2, me % 2


def score_parts(idx, lo, step):
    index = idx[...]
    step_d = jnp.zeros(index.shape, F32)
    lo_d = jnp.zeros(index.shape, F32)
    for level in range(lo.shape[0]):
        step_d = jnp.where(index == level, step[level], step_d)
        lo_d = jnp.where(index == level, lo[level], lo_d)
    high = lo_d.astype(BF16)
    rest = lo_d - high.astype(F32)
    middle = rest.astype(BF16)
    low = rest - middle.astype(F32)
    row = lax.broadcasted_iota(jnp.int32, (16, index.shape[1]), 0)
    parts = jnp.where(
        row == 0,
        high.astype(F32),
        jnp.where(row == 1, middle.astype(F32), jnp.where(row == 2, low, 0.0)),
    ).astype(BF16)
    return step_d, parts


def score(step_d, parts, own, other, member):
    contract = (((1,), (1,)), ((), ()))
    product = lambda left, right: lax.dot_general(
        left, right, contract, preferred_element_type=F32
    )
    folded = (member.astype(F32) * step_d).astype(BF16)
    most = jnp.maximum(
        jnp.max(product(own[...], folded), axis=0, keepdims=True),
        jnp.max(product(other[...], folded), axis=0, keepdims=True),
    )
    return most + jnp.sum(product(parts, member), axis=0, keepdims=True)


def near_score_kernel(idx, lo, step, own, other, u0, u1, best):
    step_d, parts = score_parts(idx, lo, step)
    members = jnp.concatenate([u0[...], u1[...]], axis=0)
    best[...] = score(step_d, parts, own, other, members)


def far_score_kernel(idx, lo, step, own, other, u0, u1, near, best):
    chip, _ = chip_and_core()
    step_d, parts = score_parts(idx, lo, step)
    members = jnp.concatenate([u0[...], u1[...]], axis=0)
    found = jnp.concatenate(
        [near[...], score(step_d, parts, own, other, members)], axis=1
    )
    total = found.shape[1]
    each = total // 16
    lane = lax.broadcasted_iota(jnp.int32, found.shape, 1)
    for bit in (1, 2, 4, 8):
        far = bit * each
        crossed = jnp.where(
            (lane // far) % 2 == 1,
            pltpu.roll(found, far, 1),
            pltpu.roll(found, total - far, 1),
        )
        found = jnp.where((chip // bit) % 2 == 1, crossed, found)
    best[...] = found


def order(slots, depth):
    chip, core = chip_and_core()
    each = depth // slots
    row = lax.broadcasted_iota(jnp.int32, (depth, depth), 0)
    slot = lax.broadcasted_iota(jnp.int32, (depth, depth), 1) // each
    place = lax.broadcasted_iota(jnp.int32, (depth, depth), 1) % each
    key = slot // 8 + 4 * ((slot // 2) % 4)
    source = ((chip ^ key) * 2 + (core + slot) % 2) * each + place
    return jnp.where(row == source, 1.0, 0.0).astype(BF16)


def hidden_kernel(slots, own, other, w0, w1, w2, w3, hidden):
    count, depth = own.shape
    pick = order(slots, depth)
    weights = jnp.concatenate([w[...] for w in (w0, w1, w2, w3)], axis=0)
    block = 256
    for start, features in ((0, own), (count, other)):
        for at in range(0, count, block):
            ordered = jnp.dot(
                features[at : at + block, :], pick, preferred_element_type=F32
            ).astype(BF16)
            v = 0.5 * jnp.dot(ordered, weights, preferred_element_type=F32)
            hidden[start + at : start + at + block, :] = (v * (1.0 + jnp.tanh(v))).astype(BF16)


def add_up(keys, mine, theirs, pieces, finish):
    chip, core = chip_and_core()
    depth = mine.shape[1]
    rows = pieces[0].shape[0] // len(keys[0])
    count = mine.shape[0]
    block = 256
    near = chip // 8 == core

    def work(first, second, first_is_mine):
        for at in range(0, count, block):
            flip = (at + count // 2) % count
            total = None
            for piece, chips in zip(pieces, keys):
                left = []
                for key in chips:
                    source = first if key < 8 else second
                    start = at if (key < 8) == first_is_mine else flip
                    column = pl.multiple_of((((chip ^ key) * rows) % depth), rows)
                    left.append(source[start : start + block, pl.ds(column, rows)])
                product = jnp.dot(
                    jnp.concatenate(left, axis=1), piece[...], preferred_element_type=F32
                )
                total = product if total is None else total + product
            finish(at, total)

    @pl.when(near)
    def _():
        work(mine, theirs, True)

    @pl.when(jnp.logical_not(near))
    def _():
        work(theirs, mine, False)


def first_embed_kernel(keys, mine, theirs, *refs):
    *pieces, partial = refs

    def finish(at, total):
        partial[at : at + total.shape[0], :] = total

    add_up(keys, mine, theirs, pieces, finish)


def last_embed_kernel(keys, mine, theirs, *refs):
    *pieces, partial, best, own, other, bounds = refs
    count = own.shape[0]
    bounds[...] = jnp.full(bounds.shape, -jnp.inf, F32)
    bounds[2:3, :] = best[...]

    def finish(at, total):
        total = total + partial[at : at + total.shape[0], :]
        if at < count:
            own[at : at + total.shape[0], :] = total
        else:
            other[at - count : at - count + total.shape[0], :] = total
        top = jnp.max(total, axis=0, keepdims=True)
        bottom = jnp.max(-total, axis=0, keepdims=True)
        bounds[0:1, :] = jnp.maximum(bounds[0:1, :], top)
        bounds[1:2, :] = jnp.maximum(bounds[1:2, :], bottom)

    add_up(keys, mine, theirs, pieces, finish)


def code_kernel(own, other, here, there, codes):
    _, core = chip_and_core()
    width = own.shape[1]
    for values, bounds, part in ((own, here, core), (other, there, 1 - core)):
        upper = bounds[0:1, :]
        lower = -bounds[1:2, :]
        mid = (upper + lower) * 0.5
        scale = 7.5 / ((upper - lower) * 0.5 + 1e-05)
        at = pl.ds(pl.multiple_of(part * width, width), width)
        codes[:, at] = ((values[...] - mid) * scale).astype(BF16)


def call(kernel, out, specs, flops, limit=24):
    outs = jax.tree.leaves(out)
    return pl.pallas_call(
        kernel,
        out_shape=out,
        in_specs=specs,
        out_specs=jax.tree.map(lambda _: VMEM, out),
        compiler_params=pltpu.CompilerParams(vmem_limit_bytes=limit * MIB),
        cost_estimate=pl.CostEstimate(
            flops=flops,
            transcendentals=0,
            bytes_accessed=sum(o.size * o.dtype.itemsize for o in outs),
        ),
    )


def shape(dims, dtype):
    return jax.ShapeDtypeStruct(dims, dtype)


def half_columns(x, core):
    width = x.shape[1] // 2
    return lax.dynamic_slice_in_dim(x, core * width, width, 1)


def most(x, others):
    for other in others:
        x = jnp.maximum(x, other)
    return x


def by_permutes(n, n_rep, items, w_in, w_out, users, res_codes, range_idx, range_lo, range_step):
    move = lambda x, k: swap(x, "fsdp", n, k)
    cat = lambda *parts: jnp.concatenate(parts, axis=0)
    chip, core = chip_and_core()
    keys = tuple(tuple(b + 4 * j for j in range(4)) for b in range(4))
    count, d_in = items.shape[1:]
    wide = w_in.shape[1] // 2
    width = w_out.shape[1] // 2

    in_rows = cat(half_columns(w_in, core), move(half_columns(w_in, 1 - core), 1))
    in_column = cat(in_rows, *(move(in_rows, k) for k in (8, 16, 24)))
    here, there = half_columns(w_out, core), move(half_columns(w_out, 1 - core), 1)
    out_rows = jnp.where(core == 0, cat(here, there), cat(there, here))
    user_pair = cat(users[0], move(users[0], 2))
    user_plane = cat(user_pair, move(user_pair, 4))
    features = items[0]
    features_other = move(features, 1)
    in_column, out_rows, features_other, resident = lax.optimization_barrier(
        (in_column, out_rows, features_other, res_codes[0])
    )

    in_pieces = [in_column] + [move(in_column, k) for k in (2, 4, 6)]
    out_far = move(out_rows, 16)
    out_column = cat(out_rows, move(out_rows, 8), out_far, move(out_far, 8))
    codes = resident.astype(BF16)
    codes_other = move(codes, 1)
    *in_pieces, out_column, user_plane = lax.optimization_barrier(
        (*in_pieces, out_column, user_plane)
    )

    hidden = call(
        functools.partial(hidden_kernel, n),
        shape((2 * count, wide), BF16),
        [VMEM] * 6,
        4 * count * d_in * wide,
    )(features, features_other, *in_pieces)
    out_x, out_y = move(out_column, 2), move(out_column, 4)
    user_near, user_far = move(user_plane, 8), move(user_plane, 16)
    out_x, out_y, user_near, user_far, hidden = lax.optimization_barrier(
        (out_x, out_y, user_near, user_far, hidden)
    )
    half = out_column.shape[0] // 2
    out_low, out_high = move(out_y[:half], 2), move(out_x[half:], 4)
    user_last = move(user_far, 8)

    ranges = (range_idx[None, :], range_lo, range_step)
    members = 2 * user_plane.shape[0]
    score_flops = 4 * members * count * users.shape[2]
    near_best = call(
        near_score_kernel,
        shape((1, members), F32),
        [VMEM, SMEM, SMEM] + [VMEM] * 4,
        score_flops,
    )(*ranges, codes, codes_other, user_plane, user_near)
    hidden_other = move(hidden, 1)
    partial = call(
        functools.partial(first_embed_kernel, keys[:3]),
        shape((2 * count, width), F32),
        [VMEM] * 5,
        6 * count * wide * width,
    )(hidden, hidden_other, out_column, out_x, out_y)
    near_best, partial = lax.optimization_barrier((near_best, partial))
    best = call(
        far_score_kernel,
        shape((1, 2 * members), F32),
        [VMEM, SMEM, SMEM] + [VMEM] * 5,
        score_flops,
    )(*ranges, codes, codes_other, user_far, user_last, near_best)

    own, other, merged = call(
        functools.partial(last_embed_kernel, (keys[3][:2], keys[3][2:])),
        (
            shape((count, width), F32),
            shape((count, width), F32),
            shape((3, width), F32),
        ),
        [VMEM] * 6,
        2 * count * wide * width,
    )(hidden, hidden_other, out_low, out_high, partial, best)
    received = move(other, 1)

    for keys in ((8, 16, 24), (2, 4, 6)):
        merged = most(merged, [move(merged, k) for k in keys])
    bounds = merged[:2]
    if n_rep > 1:
        bounds = lax.pmax(bounds, "rep")
    new_codes = call(
        code_kernel, shape((count, 2 * width), BF16), [VMEM] * 4, 4 * count * width
    )(own, received, bounds, move(bounds, 1))
    each = users.shape[1]
    mine = lax.dynamic_slice_in_dim(merged[2:], chip * each, each, 1)
    return new_codes[None], mine


def on_any(items, w_in, w_out, users, res_codes, range_idx, range_lo, range_step):
    features = items[0]
    dot = functools.partial(jnp.dot, preferred_element_type=F32)
    first = dot(features, lax.all_gather(w_in, "fsdp", axis=0, tiled=True))
    hidden = jax.nn.silu(first).astype(BF16)
    embed = dot(hidden, lax.all_gather(w_out, "fsdp", axis=0, tiled=True))
    upper = lax.pmax(jnp.max(embed, axis=0), ("fsdp", "rep"))
    lower = lax.pmin(jnp.min(embed, axis=0), ("fsdp", "rep"))
    mid = (upper + lower) * 0.5
    half = (upper - lower) * 0.5
    new_codes = (7.5 * (embed - mid) / (half + 1e-05)).astype(BF16)[None]
    levels = jnp.arange(range_lo.shape[0], dtype=jnp.int32)
    match = (range_idx[None, :] == levels[:, None]).astype(F32)
    step_d = jnp.sum(range_step[:, None] * match, axis=0)
    lo_d = jnp.sum(range_lo[:, None] * match, axis=0)
    member = lax.all_gather(users, "fsdp", axis=1, tiled=True)[0]
    folded = (member.astype(F32) * step_d).astype(BF16)
    offset = jnp.dot(member.astype(F32), lo_d, precision=lax.Precision.HIGHEST)
    scores = dot(res_codes[0].astype(BF16), folded.T)
    merged = lax.pmax((jnp.max(scores, axis=0) + offset)[None], "fsdp")
    count = users.shape[1]
    best = lax.dynamic_slice_in_dim(merged, lax.axis_index("fsdp") * count, count, 1)
    return new_codes, best


def solution(mesh):
    n = mesh.shape["fsdp"]
    body = on_any
    if n == 32:
        body = functools.partial(by_permutes, n, mesh.shape["rep"])
    return jax.shard_map(
        body,
        mesh=mesh,
        in_specs=(
            P("rep", ("grp", "fsdp"), None),
            P("fsdp", None),
            P("fsdp", None),
            P("rep", ("grp", "fsdp"), None),
            P("rep", ("grp", "fsdp"), None),
            P("grp"),
            P("grp"),
            P("grp"),
        ),
        out_specs=(P("rep", ("grp", "fsdp"), None), P("rep", ("grp", "fsdp"))),
        check_vma=False,
    )
```

```python
import functools

import jax
import jax.numpy as jnp
from jax import lax
from jax.experimental import pallas as pl
from jax.experimental.pallas import tpu as pltpu
from jax.sharding import PartitionSpec as P

VMEM = pl.BlockSpec(memory_space=pltpu.VMEM)
SMEM = pl.BlockSpec(memory_space=pltpu.SMEM)
BF16 = jnp.bfloat16
F32 = jnp.float32
MIB = 1 << 20


def swap(x, axis, n, k):
    return lax.ppermute(x, axis, [(i, i ^ k) for i in range(n)])


def chip_and_core():
    me = lax.axis_index("fsdp")
    return me // 2, me % 2


def score_parts(idx, lo, step):
    index = idx[...]
    step_d = jnp.zeros(index.shape, F32)
    lo_d = jnp.zeros(index.shape, F32)
    for level in range(lo.shape[0]):
        step_d = jnp.where(index == level, step[level], step_d)
        lo_d = jnp.where(index == level, lo[level], lo_d)
    high = lo_d.astype(BF16)
    rest = lo_d - high.astype(F32)
    middle = rest.astype(BF16)
    low = rest - middle.astype(F32)
    row = lax.broadcasted_iota(jnp.int32, (16, index.shape[1]), 0)
    parts = jnp.where(
        row == 0,
        high.astype(F32),
        jnp.where(row == 1, middle.astype(F32), jnp.where(row == 2, low, 0.0)),
    ).astype(BF16)
    return step_d, parts


def score(step_d, parts, own, other, pieces):
    chip, _ = chip_and_core()
    contract = (((1,), (1,)), ((), ()))
    product = lambda left, right: lax.dot_general(
        left, right, contract, preferred_element_type=F32
    )
    blocks = []
    for piece in pieces:
        rows = piece.shape[0] // 4
        for place in range(4):
            start = pl.multiple_of(((chip % 4) ^ place) * rows, rows)
            blocks.append(piece[pl.ds(start, rows), :])
    member = jnp.concatenate(blocks, axis=0)
    folded = (member.astype(F32) * step_d[...]).astype(BF16)
    most = jnp.maximum(
        jnp.max(product(own[...], folded), axis=0, keepdims=True),
        jnp.max(product(other[...], folded), axis=0, keepdims=True),
    )
    return most + jnp.sum(product(parts[...], member), axis=0, keepdims=True)


def near_score_kernel(step_d, parts, own, other, u0, u1, u2, best):
    best[...] = score(step_d, parts, own, other, (u0, u1, u2))


def far_score_kernel(step_d, parts, own, other, u0, near, best):
    chip, _ = chip_and_core()
    each = best.shape[1] // 4
    found = [near[:, at * each : (at + 1) * each] for at in range(3)]
    found.append(score(step_d, parts, own, other, (u0,)))
    for bit in (1, 2):
        crossed = (chip // (4 * bit)) % 2 == 1
        found = [jnp.where(crossed, found[at ^ bit], found[at]) for at in range(4)]
    for at in range(4):
        best[:, at * each : (at + 1) * each] = found[at]


def order(slots, depth):
    chip, core = chip_and_core()
    each = depth // slots
    row = lax.broadcasted_iota(jnp.int32, (depth, depth), 0)
    slot = lax.broadcasted_iota(jnp.int32, (depth, depth), 1) // each
    place = lax.broadcasted_iota(jnp.int32, (depth, depth), 1) % each
    key = slot // 8 + 4 * ((slot // 2) % 4)
    source = ((chip ^ key) * 2 + (core + slot) % 2) * each + place
    return jnp.where(row == source, 1.0, 0.0).astype(BF16)


def hidden_kernel(slots, idx, lo, step, own, other, w0, w1, w2, w3, hidden, step_d, parts):
    step_d[...], parts[...] = score_parts(idx, lo, step)
    count, depth = own.shape
    pick = order(slots, depth)
    weights = jnp.concatenate([w[...] for w in (w0, w1, w2, w3)], axis=0)
    block = 256
    for start, features in ((0, own), (count, other)):
        for at in range(0, count, block):
            ordered = jnp.dot(
                features[at : at + block, :], pick, preferred_element_type=F32
            ).astype(BF16)
            v = 0.5 * jnp.dot(ordered, weights, preferred_element_type=F32)
            hidden[start + at : start + at + block, :] = (v * (1.0 + jnp.tanh(v))).astype(BF16)


def add_up(keys, mine, theirs, pieces, finish):
    chip, core = chip_and_core()
    depth = mine.shape[1]
    rows = pieces[0].shape[0] // len(keys[0])
    count = mine.shape[0]
    block = 256
    near = chip // 8 == core

    def work(first, second, first_is_mine):
        for at in range(0, count, block):
            flip = (at + count // 2) % count
            total = None
            for piece, chips in zip(pieces, keys):
                left = []
                for key in chips:
                    source = first if key < 8 else second
                    start = at if (key < 8) == first_is_mine else flip
                    column = pl.multiple_of((((chip ^ key) * rows) % depth), rows)
                    left.append(source[start : start + block, pl.ds(column, rows)])
                product = jnp.dot(
                    jnp.concatenate(left, axis=1), piece[...], preferred_element_type=F32
                )
                total = product if total is None else total + product
            finish(at, total)

    @pl.when(near)
    def _():
        work(mine, theirs, True)

    @pl.when(jnp.logical_not(near))
    def _():
        work(theirs, mine, False)


def first_embed_kernel(keys, mine, theirs, *refs):
    *pieces, partial = refs

    def finish(at, total):
        partial[at : at + total.shape[0], :] = total

    add_up(keys, mine, theirs, pieces, finish)


def last_embed_kernel(keys, mine, theirs, *refs):
    *pieces, partial, best, own, other, bounds = refs
    count = own.shape[0]
    bounds[...] = jnp.full(bounds.shape, -jnp.inf, F32)
    bounds[2:3, :] = best[...]

    def finish(at, total):
        total = total + partial[at : at + total.shape[0], :]
        if at < count:
            own[at : at + total.shape[0], :] = total
        else:
            other[at - count : at - count + total.shape[0], :] = total
        top = jnp.max(total, axis=0, keepdims=True)
        bottom = jnp.max(-total, axis=0, keepdims=True)
        bounds[0:1, :] = jnp.maximum(bounds[0:1, :], top)
        bounds[1:2, :] = jnp.maximum(bounds[1:2, :], bottom)

    add_up(keys, mine, theirs, pieces, finish)


def code_kernel(own, other, here, there, codes):
    _, core = chip_and_core()
    width = own.shape[1]
    for values, bounds, part in ((own, here, core), (other, there, 1 - core)):
        upper = bounds[0:1, :]
        lower = -bounds[1:2, :]
        mid = (upper + lower) * 0.5
        scale = 7.5 / ((upper - lower) * 0.5 + 1e-05)
        at = pl.ds(pl.multiple_of(part * width, width), width)
        codes[:, at] = ((values[...] - mid) * scale).astype(BF16)


def call(kernel, out, specs, flops, limit=24):
    outs = jax.tree.leaves(out)
    return pl.pallas_call(
        kernel,
        out_shape=out,
        in_specs=specs,
        out_specs=jax.tree.map(lambda _: VMEM, out),
        compiler_params=pltpu.CompilerParams(vmem_limit_bytes=limit * MIB),
        cost_estimate=pl.CostEstimate(
            flops=flops,
            transcendentals=0,
            bytes_accessed=sum(o.size * o.dtype.itemsize for o in outs),
        ),
    )


def shape(dims, dtype):
    return jax.ShapeDtypeStruct(dims, dtype)


def half_columns(x, core):
    width = x.shape[1] // 2
    return lax.dynamic_slice_in_dim(x, core * width, width, 1)


def most(x, others):
    for other in others:
        x = jnp.maximum(x, other)
    return x


def by_permutes(n, n_rep, items, w_in, w_out, users, res_codes, range_idx, range_lo, range_step):
    move = lambda x, k: swap(x, "fsdp", n, k)
    cat = lambda *parts: jnp.concatenate(parts, axis=0)
    chip, core = chip_and_core()
    keys = tuple(tuple(b + 4 * j for j in range(4)) for b in range(4))
    count, d_in = items.shape[1:]
    wide = w_in.shape[1] // 2
    width = w_out.shape[1] // 2

    in_rows = cat(half_columns(w_in, core), move(half_columns(w_in, 1 - core), 1))
    in_column = cat(in_rows, *(move(in_rows, k) for k in (8, 16, 24)))
    here, there = half_columns(w_out, core), move(half_columns(w_out, 1 - core), 1)
    out_rows = jnp.where(core == 0, cat(here, there), cat(there, here))
    user_pair = cat(users[0], move(users[0], 2))
    user_plane = cat(user_pair, move(user_pair, 4))
    features = items[0]
    features_other = move(features, 1)
    in_column, out_rows, features_other, resident = lax.optimization_barrier(
        (in_column, out_rows, features_other, res_codes[0])
    )

    in_pieces = [in_column] + [move(in_column, k) for k in (2, 4, 6)]
    out_far = move(out_rows, 16)
    out_column = cat(out_rows, move(out_rows, 8), out_far, move(out_far, 8))
    codes = resident.astype(BF16)
    codes_other = move(codes, 1)
    *in_pieces, out_column, user_plane = lax.optimization_barrier(
        (*in_pieces, out_column, user_plane)
    )

    dims = users.shape[2]
    hidden, *ranges = call(
        functools.partial(hidden_kernel, n),
        (shape((2 * count, wide), BF16), shape((1, dims), F32), shape((16, dims), BF16)),
        [VMEM, SMEM, SMEM] + [VMEM] * 6,
        4 * count * d_in * wide,
    )(range_idx[None, :], range_lo, range_step, features, features_other, *in_pieces)
    out_x, out_y = move(out_column, 2), move(out_column, 4)
    user_near, user_far = move(user_plane, 8), move(user_plane, 16)
    out_x, out_y, user_near, user_far, hidden = lax.optimization_barrier(
        (out_x, out_y, user_near, user_far, hidden)
    )
    half = out_column.shape[0] // 2
    out_low, out_high = move(out_y[:half], 2), move(out_x[half:], 4)
    user_last = move(user_far, 8)

    members = user_plane.shape[0]
    score_flops = 4 * members * count * dims
    hidden_other = move(hidden, 1)
    partial = call(
        functools.partial(first_embed_kernel, keys[:3]),
        shape((2 * count, width), F32),
        [VMEM] * 5,
        6 * count * wide * width,
    )(hidden, hidden_other, out_column, out_x, out_y)
    near_plane, partial = lax.optimization_barrier((user_plane, partial))
    near_best = call(
        near_score_kernel,
        shape((1, 3 * members), F32),
        [VMEM] * 7,
        3 * score_flops,
    )(*ranges, codes, codes_other, near_plane, user_near, user_far)
    best = call(
        far_score_kernel,
        shape((1, 4 * members), F32),
        [VMEM] * 6,
        score_flops,
    )(*ranges, codes, codes_other, user_last, near_best)

    own, other, merged = call(
        functools.partial(last_embed_kernel, (keys[3][:2], keys[3][2:])),
        (
            shape((count, width), F32),
            shape((count, width), F32),
            shape((3, width), F32),
        ),
        [VMEM] * 6,
        2 * count * wide * width,
    )(hidden, hidden_other, out_low, out_high, partial, best)
    received = move(other, 1)

    for keys in ((8, 16, 24), (2, 4, 6)):
        merged = most(merged, [move(merged, k) for k in keys])
    bounds = merged[:2]
    if n_rep > 1:
        bounds = lax.pmax(bounds, "rep")
    new_codes = call(
        code_kernel, shape((count, 2 * width), BF16), [VMEM] * 4, 4 * count * width
    )(own, received, bounds, move(bounds, 1))
    each = users.shape[1]
    mine = lax.dynamic_slice_in_dim(merged[2:], chip * each, each, 1)
    return new_codes[None], mine


def on_any(items, w_in, w_out, users, res_codes, range_idx, range_lo, range_step):
    features = items[0]
    dot = functools.partial(jnp.dot, preferred_element_type=F32)
    first = dot(features, lax.all_gather(w_in, "fsdp", axis=0, tiled=True))
    hidden = jax.nn.silu(first).astype(BF16)
    embed = dot(hidden, lax.all_gather(w_out, "fsdp", axis=0, tiled=True))
    upper = lax.pmax(jnp.max(embed, axis=0), ("fsdp", "rep"))
    lower = lax.pmin(jnp.min(embed, axis=0), ("fsdp", "rep"))
    mid = (upper + lower) * 0.5
    half = (upper - lower) * 0.5
    new_codes = (7.5 * (embed - mid) / (half + 1e-05)).astype(BF16)[None]
    levels = jnp.arange(range_lo.shape[0], dtype=jnp.int32)
    match = (range_idx[None, :] == levels[:, None]).astype(F32)
    step_d = jnp.sum(range_step[:, None] * match, axis=0)
    lo_d = jnp.sum(range_lo[:, None] * match, axis=0)
    member = lax.all_gather(users, "fsdp", axis=1, tiled=True)[0]
    folded = (member.astype(F32) * step_d).astype(BF16)
    offset = jnp.dot(member.astype(F32), lo_d, precision=lax.Precision.HIGHEST)
    scores = dot(res_codes[0].astype(BF16), folded.T)
    merged = lax.pmax((jnp.max(scores, axis=0) + offset)[None], "fsdp")
    count = users.shape[1]
    best = lax.dynamic_slice_in_dim(merged, lax.axis_index("fsdp") * count, count, 1)
    return new_codes, best


def solution(mesh):
    n = mesh.shape["fsdp"]
    body = on_any
    if n == 32:
        body = functools.partial(by_permutes, n, mesh.shape["rep"])
    return jax.shard_map(
        body,
        mesh=mesh,
        in_specs=(
            P("rep", ("grp", "fsdp"), None),
            P("fsdp", None),
            P("fsdp", None),
            P("rep", ("grp", "fsdp"), None),
            P("rep", ("grp", "fsdp"), None),
            P("grp"),
            P("grp"),
            P("grp"),
        ),
        out_specs=(P("rep", ("grp", "fsdp"), None), P("rep", ("grp", "fsdp"))),
        check_vma=False,
    )
```

```python
import functools

import jax
import jax.numpy as jnp
from jax import lax
from jax.experimental import pallas as pl
from jax.experimental.pallas import tpu as pltpu
from jax.sharding import PartitionSpec as P

VMEM = pl.BlockSpec(memory_space=pltpu.VMEM)
SMEM = pl.BlockSpec(memory_space=pltpu.SMEM)
BF16 = jnp.bfloat16
F32 = jnp.float32
MIB = 1 << 20


def swap(x, axis, n, k):
    return lax.ppermute(x, axis, [(i, i ^ k) for i in range(n)])


def chip_and_core():
    me = lax.axis_index("fsdp")
    return me // 2, me % 2


def score_parts(idx, lo, step):
    index = idx[...]
    step_d = jnp.zeros(index.shape, F32)
    lo_d = jnp.zeros(index.shape, F32)
    for level in range(lo.shape[0]):
        step_d = jnp.where(index == level, step[level], step_d)
        lo_d = jnp.where(index == level, lo[level], lo_d)
    high = lo_d.astype(BF16)
    rest = lo_d - high.astype(F32)
    middle = rest.astype(BF16)
    low = rest - middle.astype(F32)
    row = lax.broadcasted_iota(jnp.int32, (16, index.shape[1]), 0)
    parts = jnp.where(
        row == 0,
        high.astype(F32),
        jnp.where(row == 1, middle.astype(F32), jnp.where(row == 2, low, 0.0)),
    ).astype(BF16)
    return step_d, parts


def score(step_d, parts, own, other, pieces):
    chip, _ = chip_and_core()
    contract = (((1,), (1,)), ((), ()))
    product = lambda left, right: lax.dot_general(
        left, right, contract, preferred_element_type=F32
    )
    blocks = []
    for piece in pieces:
        rows = piece.shape[0] // 4
        for place in range(4):
            start = pl.multiple_of(((chip % 4) ^ place) * rows, rows)
            blocks.append(piece[pl.ds(start, rows), :])
    member = jnp.concatenate(blocks, axis=0)
    folded = (member.astype(F32) * step_d[...]).astype(BF16)
    most = jnp.maximum(
        jnp.max(product(own[...], folded), axis=0, keepdims=True),
        jnp.max(product(other[...], folded), axis=0, keepdims=True),
    )
    return most + jnp.sum(product(parts[...], member), axis=0, keepdims=True)


def near_score_kernel(step_d, parts, own, other, u0, u1, u2, best):
    best[...] = score(step_d, parts, own, other, (u0, u1, u2))


def far_score_kernel(step_d, parts, own, other, u0, near, best):
    chip, _ = chip_and_core()
    each = best.shape[1] // 4
    found = [near[:, at * each : (at + 1) * each] for at in range(3)]
    found.append(score(step_d, parts, own, other, (u0,)))
    for bit in (1, 2):
        crossed = (chip // (4 * bit)) % 2 == 1
        found = [jnp.where(crossed, found[at ^ bit], found[at]) for at in range(4)]
    for at in range(4):
        best[:, at * each : (at + 1) * each] = found[at]


def order(slots, depth):
    chip, core = chip_and_core()
    each = depth // slots
    row = lax.broadcasted_iota(jnp.int32, (depth, depth), 0)
    slot = lax.broadcasted_iota(jnp.int32, (depth, depth), 1) // each
    place = lax.broadcasted_iota(jnp.int32, (depth, depth), 1) % each
    key = slot // 8 + 4 * ((slot // 2) % 4)
    source = ((chip ^ key) * 2 + (core + slot) % 2) * each + place
    return jnp.where(row == source, 1.0, 0.0).astype(BF16)


def hidden_kernel(slots, idx, lo, step, own, other, w0, w1, w2, w3, hidden, step_d, parts):
    step_d[...], parts[...] = score_parts(idx, lo, step)
    count, depth = own.shape
    pick = order(slots, depth)
    weights = jnp.concatenate([w[...] for w in (w0, w1, w2, w3)], axis=0)
    block = 256
    for start, features in ((0, own), (count, other)):
        for at in range(0, count, block):
            ordered = jnp.dot(
                features[at : at + block, :], pick, preferred_element_type=F32
            ).astype(BF16)
            v = 0.5 * jnp.dot(ordered, weights, preferred_element_type=F32)
            hidden[start + at : start + at + block, :] = (v * (1.0 + jnp.tanh(v))).astype(BF16)


def add_up(keys, mine, theirs, pieces, finish):
    chip, core = chip_and_core()
    depth = mine.shape[1]
    rows = pieces[0].shape[0] // len(keys[0])
    count = mine.shape[0]
    block = 256
    near = chip // 8 == core

    def work(first, second, first_is_mine):
        for at in range(0, count, block):
            flip = (at + count // 2) % count
            total = None
            for piece, chips in zip(pieces, keys):
                left = []
                for key in chips:
                    source = first if key < 8 else second
                    start = at if (key < 8) == first_is_mine else flip
                    column = pl.multiple_of((((chip ^ key) * rows) % depth), rows)
                    left.append(source[start : start + block, pl.ds(column, rows)])
                product = jnp.dot(
                    jnp.concatenate(left, axis=1), piece[...], preferred_element_type=F32
                )
                total = product if total is None else total + product
            finish(at, total)

    @pl.when(near)
    def _():
        work(mine, theirs, True)

    @pl.when(jnp.logical_not(near))
    def _():
        work(theirs, mine, False)


def first_embed_kernel(keys, mine, theirs, *refs):
    *pieces, partial = refs

    def finish(at, total):
        partial[at : at + total.shape[0], :] = total

    add_up(keys, mine, theirs, pieces, finish)


def last_embed_kernel(keys, mine, theirs, *refs):
    *pieces, partial, best, own, other, bounds = refs
    count = own.shape[0]
    bounds[...] = jnp.full(bounds.shape, -jnp.inf, F32)
    bounds[2:3, :] = best[...]

    def finish(at, total):
        total = total + partial[at : at + total.shape[0], :]
        if at < count:
            own[at : at + total.shape[0], :] = total
        else:
            other[at - count : at - count + total.shape[0], :] = total
        top = jnp.max(total, axis=0, keepdims=True)
        bottom = jnp.max(-total, axis=0, keepdims=True)
        bounds[0:1, :] = jnp.maximum(bounds[0:1, :], top)
        bounds[1:2, :] = jnp.maximum(bounds[1:2, :], bottom)

    add_up(keys, mine, theirs, pieces, finish)


def code_kernel(own, other, here, there, codes):
    _, core = chip_and_core()
    width = own.shape[1]
    for values, bounds, part in ((own, here, core), (other, there, 1 - core)):
        upper = bounds[0:1, :]
        lower = -bounds[1:2, :]
        mid = (upper + lower) * 0.5
        scale = 7.5 / ((upper - lower) * 0.5 + 1e-05)
        at = pl.ds(pl.multiple_of(part * width, width), width)
        codes[:, at] = ((values[...] - mid) * scale).astype(BF16)


def call(kernel, out, specs, flops, limit=24):
    outs = jax.tree.leaves(out)
    return pl.pallas_call(
        kernel,
        out_shape=out,
        in_specs=specs,
        out_specs=jax.tree.map(lambda _: VMEM, out),
        compiler_params=pltpu.CompilerParams(vmem_limit_bytes=limit * MIB),
        cost_estimate=pl.CostEstimate(
            flops=flops,
            transcendentals=0,
            bytes_accessed=sum(o.size * o.dtype.itemsize for o in outs),
        ),
    )


def shape(dims, dtype):
    return jax.ShapeDtypeStruct(dims, dtype)


def half_columns(x, core):
    width = x.shape[1] // 2
    return lax.dynamic_slice_in_dim(x, core * width, width, 1)


def most(x, others):
    for other in others:
        x = jnp.maximum(x, other)
    return x


def by_permutes(n, n_rep, items, w_in, w_out, users, res_codes, range_idx, range_lo, range_step):
    move = lambda x, k: swap(x, "fsdp", n, k)
    cat = lambda *parts: jnp.concatenate(parts, axis=0)
    chip, core = chip_and_core()
    keys = tuple(tuple(b + 4 * j for j in range(4)) for b in range(4))
    count, d_in = items.shape[1:]
    wide = w_in.shape[1] // 2
    width = w_out.shape[1] // 2

    in_rows = cat(half_columns(w_in, core), move(half_columns(w_in, 1 - core), 1))
    in_column = cat(in_rows, *(move(in_rows, k) for k in (8, 16, 24)))
    w_out, in_rows = lax.optimization_barrier((w_out, in_rows))
    here, there = half_columns(w_out, core), move(half_columns(w_out, 1 - core), 1)
    out_rows = jnp.where(core == 0, cat(here, there), cat(there, here))
    user_pair = cat(users[0], move(users[0], 2))
    user_plane = cat(user_pair, move(user_pair, 4))
    features = items[0]
    features_other = move(features, 1)
    in_column, out_rows, features_other, resident = lax.optimization_barrier(
        (in_column, out_rows, features_other, res_codes[0])
    )

    in_pieces = [in_column] + [move(in_column, k) for k in (2, 4, 6)]
    out_far = move(out_rows, 16)
    out_column = cat(out_rows, move(out_rows, 8), out_far, move(out_far, 8))
    codes = resident.astype(BF16)
    codes_other = move(codes, 1)
    *in_pieces, out_column, user_plane = lax.optimization_barrier(
        (*in_pieces, out_column, user_plane)
    )

    dims = users.shape[2]
    hidden, *ranges = call(
        functools.partial(hidden_kernel, n),
        (shape((2 * count, wide), BF16), shape((1, dims), F32), shape((16, dims), BF16)),
        [VMEM, SMEM, SMEM] + [VMEM] * 6,
        4 * count * d_in * wide,
    )(range_idx[None, :], range_lo, range_step, features, features_other, *in_pieces)
    out_x, out_y = move(out_column, 2), move(out_column, 4)
    user_near, user_far = move(user_plane, 8), move(user_plane, 16)
    out_x, out_y, user_near, user_far, hidden = lax.optimization_barrier(
        (out_x, out_y, user_near, user_far, hidden)
    )
    half = out_column.shape[0] // 2
    out_low, out_high = move(out_y[:half], 2), move(out_x[half:], 4)
    user_last = move(user_far, 8)

    members = user_plane.shape[0]
    score_flops = 4 * members * count * dims
    hidden_other = move(hidden, 1)
    partial = call(
        functools.partial(first_embed_kernel, keys[:3]),
        shape((2 * count, width), F32),
        [VMEM] * 5,
        6 * count * wide * width,
    )(hidden, hidden_other, out_column, out_x, out_y)
    near_plane, partial = lax.optimization_barrier((user_plane, partial))
    near_best = call(
        near_score_kernel,
        shape((1, 3 * members), F32),
        [VMEM] * 7,
        3 * score_flops,
    )(*ranges, codes, codes_other, near_plane, user_near, user_far)
    best = call(
        far_score_kernel,
        shape((1, 4 * members), F32),
        [VMEM] * 6,
        score_flops,
    )(*ranges, codes, codes_other, user_last, near_best)

    own, other, merged = call(
        functools.partial(last_embed_kernel, (keys[3][:2], keys[3][2:])),
        (
            shape((count, width), F32),
            shape((count, width), F32),
            shape((3, width), F32),
        ),
        [VMEM] * 6,
        2 * count * wide * width,
    )(hidden, hidden_other, out_low, out_high, partial, best)
    received = move(other, 1)

    for keys in ((8, 16, 24), (2, 4, 6)):
        merged = most(merged, [move(merged, k) for k in keys])
    bounds = merged[:2]
    if n_rep > 1:
        bounds = lax.pmax(bounds, "rep")
    new_codes = call(
        code_kernel, shape((count, 2 * width), BF16), [VMEM] * 4, 4 * count * width
    )(own, received, bounds, move(bounds, 1))
    each = users.shape[1]
    mine = lax.dynamic_slice_in_dim(merged[2:], chip * each, each, 1)
    return new_codes[None], mine


def on_any(items, w_in, w_out, users, res_codes, range_idx, range_lo, range_step):
    features = items[0]
    dot = functools.partial(jnp.dot, preferred_element_type=F32)
    first = dot(features, lax.all_gather(w_in, "fsdp", axis=0, tiled=True))
    hidden = jax.nn.silu(first).astype(BF16)
    embed = dot(hidden, lax.all_gather(w_out, "fsdp", axis=0, tiled=True))
    upper = lax.pmax(jnp.max(embed, axis=0), ("fsdp", "rep"))
    lower = lax.pmin(jnp.min(embed, axis=0), ("fsdp", "rep"))
    mid = (upper + lower) * 0.5
    half = (upper - lower) * 0.5
    new_codes = (7.5 * (embed - mid) / (half + 1e-05)).astype(BF16)[None]
    levels = jnp.arange(range_lo.shape[0], dtype=jnp.int32)
    match = (range_idx[None, :] == levels[:, None]).astype(F32)
    step_d = jnp.sum(range_step[:, None] * match, axis=0)
    lo_d = jnp.sum(range_lo[:, None] * match, axis=0)
    member = lax.all_gather(users, "fsdp", axis=1, tiled=True)[0]
    folded = (member.astype(F32) * step_d).astype(BF16)
    offset = jnp.dot(member.astype(F32), lo_d, precision=lax.Precision.HIGHEST)
    scores = dot(res_codes[0].astype(BF16), folded.T)
    merged = lax.pmax((jnp.max(scores, axis=0) + offset)[None], "fsdp")
    count = users.shape[1]
    best = lax.dynamic_slice_in_dim(merged, lax.axis_index("fsdp") * count, count, 1)
    return new_codes, best


def solution(mesh):
    n = mesh.shape["fsdp"]
    body = on_any
    if n == 32:
        body = functools.partial(by_permutes, n, mesh.shape["rep"])
    return jax.shard_map(
        body,
        mesh=mesh,
        in_specs=(
            P("rep", ("grp", "fsdp"), None),
            P("fsdp", None),
            P("fsdp", None),
            P("rep", ("grp", "fsdp"), None),
            P("rep", ("grp", "fsdp"), None),
            P("grp"),
            P("grp"),
            P("grp"),
        ),
        out_specs=(P("rep", ("grp", "fsdp"), None), P("rep", ("grp", "fsdp"))),
        check_vma=False,
    )
```

```python
import functools

import jax
import jax.numpy as jnp
from jax import lax
from jax.experimental import pallas as pl
from jax.experimental.pallas import tpu as pltpu
from jax.sharding import PartitionSpec as P

VMEM = pl.BlockSpec(memory_space=pltpu.VMEM)
SMEM = pl.BlockSpec(memory_space=pltpu.SMEM)
BF16 = jnp.bfloat16
F32 = jnp.float32
MIB = 1 << 20


def swap(x, axis, n, k):
    return lax.ppermute(x, axis, [(i, i ^ k) for i in range(n)])


def chip_and_core():
    me = lax.axis_index("fsdp")
    return me // 2, me % 2


def score_parts(idx, lo, step):
    index = idx[...]
    step_d = jnp.zeros(index.shape, F32)
    lo_d = jnp.zeros(index.shape, F32)
    for level in range(lo.shape[0]):
        step_d = jnp.where(index == level, step[level], step_d)
        lo_d = jnp.where(index == level, lo[level], lo_d)
    high = lo_d.astype(BF16)
    rest = lo_d - high.astype(F32)
    middle = rest.astype(BF16)
    low = rest - middle.astype(F32)
    row = lax.broadcasted_iota(jnp.int32, (16, index.shape[1]), 0)
    parts = jnp.where(
        row == 0,
        high.astype(F32),
        jnp.where(row == 1, middle.astype(F32), jnp.where(row == 2, low, 0.0)),
    ).astype(BF16)
    return step_d, parts


def score(step_d, parts, own, other, pieces):
    chip, _ = chip_and_core()
    contract = (((1,), (1,)), ((), ()))
    product = lambda left, right: lax.dot_general(
        left, right, contract, preferred_element_type=F32
    )
    blocks = []
    for piece in pieces:
        rows = piece.shape[0] // 4
        for place in range(4):
            start = pl.multiple_of(((chip % 4) ^ place) * rows, rows)
            blocks.append(piece[pl.ds(start, rows), :])
    member = jnp.concatenate(blocks, axis=0)
    folded = (member.astype(F32) * step_d[...]).astype(BF16)
    most = jnp.maximum(
        jnp.max(product(own[...], folded), axis=0, keepdims=True),
        jnp.max(product(other[...], folded), axis=0, keepdims=True),
    )
    return most + jnp.sum(product(parts[...], member), axis=0, keepdims=True)


def near_score_kernel(step_d, parts, own, other, u0, u1, u2, best):
    best[...] = score(step_d, parts, own, other, (u0, u1, u2))


def far_score_kernel(step_d, parts, own, other, u0, near, best):
    chip, _ = chip_and_core()
    each = best.shape[1] // 4
    found = [near[:, at * each : (at + 1) * each] for at in range(3)]
    found.append(score(step_d, parts, own, other, (u0,)))
    for bit in (1, 2):
        crossed = (chip // (4 * bit)) % 2 == 1
        found = [jnp.where(crossed, found[at ^ bit], found[at]) for at in range(4)]
    for at in range(4):
        best[:, at * each : (at + 1) * each] = found[at]


def order(slots, depth):
    chip, core = chip_and_core()
    each = depth // slots
    row = lax.broadcasted_iota(jnp.int32, (depth, depth), 0)
    slot = lax.broadcasted_iota(jnp.int32, (depth, depth), 1) // each
    place = lax.broadcasted_iota(jnp.int32, (depth, depth), 1) % each
    key = slot // 8 + 4 * ((slot // 2) % 4)
    source = ((chip ^ key) * 2 + (core + slot) % 2) * each + place
    return jnp.where(row == source, 1.0, 0.0).astype(BF16)


def hidden_kernel(slots, idx, lo, step, own, other, w0, w1, w2, w3, hidden, step_d, parts):
    step_d[...], parts[...] = score_parts(idx, lo, step)
    count, depth = own.shape
    pick = order(slots, depth)
    weights = jnp.concatenate([w[...] for w in (w0, w1, w2, w3)], axis=0)
    block = 256
    for start, features in ((0, own), (count, other)):
        for at in range(0, count, block):
            ordered = jnp.dot(
                features[at : at + block, :], pick, preferred_element_type=F32
            ).astype(BF16)
            v = 0.5 * jnp.dot(ordered, weights, preferred_element_type=F32)
            hidden[start + at : start + at + block, :] = (v * (1.0 + jnp.tanh(v))).astype(BF16)


def add_up(keys, mine, theirs, pieces, finish):
    chip, core = chip_and_core()
    depth = mine.shape[1]
    rows = pieces[0].shape[0] // len(keys[0])
    count = mine.shape[0]
    block = 256
    near = chip // 8 == core

    def work(first, second, first_is_mine):
        for at in range(0, count, block):
            flip = (at + count // 2) % count
            total = None
            for piece, chips in zip(pieces, keys):
                left = []
                for key in chips:
                    source = first if key < 8 else second
                    start = at if (key < 8) == first_is_mine else flip
                    column = pl.multiple_of((((chip ^ key) * rows) % depth), rows)
                    left.append(source[start : start + block, pl.ds(column, rows)])
                product = jnp.dot(
                    jnp.concatenate(left, axis=1), piece[...], preferred_element_type=F32
                )
                total = product if total is None else total + product
            finish(at, total)

    @pl.when(near)
    def _():
        work(mine, theirs, True)

    @pl.when(jnp.logical_not(near))
    def _():
        work(theirs, mine, False)


def first_embed_kernel(keys, mine, theirs, *refs):
    *pieces, partial = refs

    def finish(at, total):
        partial[at : at + total.shape[0], :] = total

    add_up(keys, mine, theirs, pieces, finish)


def last_embed_kernel(keys, mine, theirs, *refs):
    *pieces, partial, best, own, other, bounds = refs
    count = own.shape[0]
    bounds[...] = jnp.full(bounds.shape, -jnp.inf, F32)
    bounds[2:3, :] = best[...]

    def finish(at, total):
        total = total + partial[at : at + total.shape[0], :]
        if at < count:
            own[at : at + total.shape[0], :] = total
        else:
            other[at - count : at - count + total.shape[0], :] = total
        top = jnp.max(total, axis=0, keepdims=True)
        bottom = jnp.max(-total, axis=0, keepdims=True)
        bounds[0:1, :] = jnp.maximum(bounds[0:1, :], top)
        bounds[1:2, :] = jnp.maximum(bounds[1:2, :], bottom)

    add_up(keys, mine, theirs, pieces, finish)


def code_kernel(own, other, here, there, codes, held, sems):
    _, core = chip_and_core()
    count, width = own.shape
    block = count // 4
    ranges = []
    for bounds in (here, there):
        upper = bounds[0:1, :]
        lower = -bounds[1:2, :]
        ranges.append(
            ((upper + lower) * 0.5, 7.5 / ((upper - lower) * 0.5 + 1e-05))
        )
    copies = []
    for step in range(4):
        rows = pl.ds(step * block, block)
        for values, (mid, scale), part in zip((own, other), ranges, (core, 1 - core)):
            at = pl.ds(pl.multiple_of(part * width, width), width)
            held[rows, at] = ((values[rows, :] - mid) * scale).astype(BF16)
        copies.append(
            pltpu.make_async_copy(held.at[rows, :], codes.at[rows, :], sems.at[step])
        )
        copies[-1].start()
    for copy in copies:
        copy.wait()


def call(kernel, out, specs, flops, limit=24):
    outs = jax.tree.leaves(out)
    return pl.pallas_call(
        kernel,
        out_shape=out,
        in_specs=specs,
        out_specs=jax.tree.map(lambda _: VMEM, out),
        compiler_params=pltpu.CompilerParams(vmem_limit_bytes=limit * MIB),
        cost_estimate=pl.CostEstimate(
            flops=flops,
            transcendentals=0,
            bytes_accessed=sum(o.size * o.dtype.itemsize for o in outs),
        ),
    )


def shape(dims, dtype):
    return jax.ShapeDtypeStruct(dims, dtype)


def half_columns(x, core):
    width = x.shape[1] // 2
    return lax.dynamic_slice_in_dim(x, core * width, width, 1)


def most(x, others):
    for other in others:
        x = jnp.maximum(x, other)
    return x


def by_permutes(n, n_rep, items, w_in, w_out, users, res_codes, range_idx, range_lo, range_step):
    move = lambda x, k: swap(x, "fsdp", n, k)
    cat = lambda *parts: jnp.concatenate(parts, axis=0)
    chip, core = chip_and_core()
    keys = tuple(tuple(b + 4 * j for j in range(4)) for b in range(4))
    count, d_in = items.shape[1:]
    wide = w_in.shape[1] // 2
    width = w_out.shape[1] // 2

    in_rows = cat(half_columns(w_in, core), move(half_columns(w_in, 1 - core), 1))
    in_column = cat(in_rows, *(move(in_rows, k) for k in (8, 16, 24)))
    w_out, in_rows = lax.optimization_barrier((w_out, in_rows))
    here, there = half_columns(w_out, core), move(half_columns(w_out, 1 - core), 1)
    out_rows = jnp.where(core == 0, cat(here, there), cat(there, here))
    user_pair = cat(users[0], move(users[0], 2))
    user_plane = cat(user_pair, move(user_pair, 4))
    features = items[0]
    features_other = move(features, 1)
    in_column, out_rows, features_other, resident = lax.optimization_barrier(
        (in_column, out_rows, features_other, res_codes[0])
    )

    in_pieces = [in_column] + [move(in_column, k) for k in (2, 4, 6)]
    out_far = move(out_rows, 16)
    out_column = cat(out_rows, move(out_rows, 8), out_far, move(out_far, 8))
    codes = resident.astype(BF16)
    codes_other = move(codes, 1)
    *in_pieces, out_column, user_plane = lax.optimization_barrier(
        (*in_pieces, out_column, user_plane)
    )

    dims = users.shape[2]
    hidden, *ranges = call(
        functools.partial(hidden_kernel, n),
        (shape((2 * count, wide), BF16), shape((1, dims), F32), shape((16, dims), BF16)),
        [VMEM, SMEM, SMEM] + [VMEM] * 6,
        4 * count * d_in * wide,
    )(range_idx[None, :], range_lo, range_step, features, features_other, *in_pieces)
    out_x, out_y = move(out_column, 2), move(out_column, 4)
    user_near, user_far = move(user_plane, 8), move(user_plane, 16)
    out_x, out_y, user_near, user_far, hidden = lax.optimization_barrier(
        (out_x, out_y, user_near, user_far, hidden)
    )
    half = out_column.shape[0] // 2
    out_low, out_high = move(out_y[:half], 2), move(out_x[half:], 4)
    user_last = move(user_far, 8)

    members = user_plane.shape[0]
    score_flops = 4 * members * count * dims
    hidden_other = move(hidden, 1)
    partial = call(
        functools.partial(first_embed_kernel, keys[:3]),
        shape((2 * count, width), F32),
        [VMEM] * 5,
        6 * count * wide * width,
    )(hidden, hidden_other, out_column, out_x, out_y)
    near_plane, partial = lax.optimization_barrier((user_plane, partial))
    near_best = call(
        near_score_kernel,
        shape((1, 3 * members), F32),
        [VMEM] * 7,
        3 * score_flops,
    )(*ranges, codes, codes_other, near_plane, user_near, user_far)
    best = call(
        far_score_kernel,
        shape((1, 4 * members), F32),
        [VMEM] * 6,
        score_flops,
    )(*ranges, codes, codes_other, user_last, near_best)

    own, other, merged = call(
        functools.partial(last_embed_kernel, (keys[3][:2], keys[3][2:])),
        (
            shape((count, width), F32),
            shape((count, width), F32),
            shape((3, width), F32),
        ),
        [VMEM] * 6,
        2 * count * wide * width,
    )(hidden, hidden_other, out_low, out_high, partial, best)
    received = move(other, 1)

    for keys in ((8, 16, 24), (2, 4, 6)):
        merged = most(merged, [move(merged, k) for k in keys])
    bounds = merged[:2]
    if n_rep > 1:
        bounds = lax.pmax(bounds, "rep")
    new_codes = pl.pallas_call(
        code_kernel,
        out_shape=shape((count, 2 * width), BF16),
        in_specs=[VMEM] * 4,
        out_specs=pl.BlockSpec(memory_space=pl.ANY),
        scratch_shapes=[
            pltpu.VMEM((count, 2 * width), BF16),
            pltpu.SemaphoreType.DMA((4,)),
        ],
        compiler_params=pltpu.CompilerParams(vmem_limit_bytes=24 * MIB),
    )(own, received, bounds, move(bounds, 1))
    each = users.shape[1]
    mine = lax.dynamic_slice_in_dim(merged[2:], chip * each, each, 1)
    return new_codes[None], mine


def on_any(items, w_in, w_out, users, res_codes, range_idx, range_lo, range_step):
    features = items[0]
    dot = functools.partial(jnp.dot, preferred_element_type=F32)
    first = dot(features, lax.all_gather(w_in, "fsdp", axis=0, tiled=True))
    hidden = jax.nn.silu(first).astype(BF16)
    embed = dot(hidden, lax.all_gather(w_out, "fsdp", axis=0, tiled=True))
    upper = lax.pmax(jnp.max(embed, axis=0), ("fsdp", "rep"))
    lower = lax.pmin(jnp.min(embed, axis=0), ("fsdp", "rep"))
    mid = (upper + lower) * 0.5
    half = (upper - lower) * 0.5
    new_codes = (7.5 * (embed - mid) / (half + 1e-05)).astype(BF16)[None]
    levels = jnp.arange(range_lo.shape[0], dtype=jnp.int32)
    match = (range_idx[None, :] == levels[:, None]).astype(F32)
    step_d = jnp.sum(range_step[:, None] * match, axis=0)
    lo_d = jnp.sum(range_lo[:, None] * match, axis=0)
    member = lax.all_gather(users, "fsdp", axis=1, tiled=True)[0]
    folded = (member.astype(F32) * step_d).astype(BF16)
    offset = jnp.dot(member.astype(F32), lo_d, precision=lax.Precision.HIGHEST)
    scores = dot(res_codes[0].astype(BF16), folded.T)
    merged = lax.pmax((jnp.max(scores, axis=0) + offset)[None], "fsdp")
    count = users.shape[1]
    best = lax.dynamic_slice_in_dim(merged, lax.axis_index("fsdp") * count, count, 1)
    return new_codes, best


def solution(mesh):
    n = mesh.shape["fsdp"]
    body = on_any
    if n == 32:
        body = functools.partial(by_permutes, n, mesh.shape["rep"])
    return jax.shard_map(
        body,
        mesh=mesh,
        in_specs=(
            P("rep", ("grp", "fsdp"), None),
            P("fsdp", None),
            P("fsdp", None),
            P("rep", ("grp", "fsdp"), None),
            P("rep", ("grp", "fsdp"), None),
            P("grp"),
            P("grp"),
            P("grp"),
        ),
        out_specs=(P("rep", ("grp", "fsdp"), None), P("rep", ("grp", "fsdp"))),
        check_vma=False,
    )
```
